512 devices in a mesh: row: 16 (over y, core), col: 32 (over z, x).
Axes of the slice: x: 4, y: 8, z: 8, core: 2. Of those that a mesh axis runs over, the one named last changes fastest.
Arguments:
- stored_inverse: bfloat16 [6, 16, 3, 32, 256, 256], P(None, 'row', None, 'col'), may hold values from -6 to 6
- panel_first: bfloat16 [6, 16, 256, 256], P(None, 'row', 'col'), may hold values from -0.046875 to 0.046875
- panel_second: bfloat16 [6, 16, 256, 256], P(None, 'row', 'col'), may hold values from -0.0546875 to 0.0546875
- panel_link: bfloat16 [256, 256], replicated, may hold values from -0.375 to 0.375
- inv_first: float32 [256, 256], replicated, as said below
- inv_second: float32 [256, 256], replicated, as said below
- struct_first: int32 [72], replicated, may hold values from 0 to 95, as said below
- struct_second: int32 [48], replicated, may hold values from 0 to 95, as said below
Outputs:
- column_first: float32 [6, 16, 256, 256], P(None, 'row', 'col')
- column_second: float32 [6, 16, 256, 256], P(None, 'row', 'col')
- diag_first: float32 [256, 256], P('col')
- link_block: float32 [256, 256], P('col')
- diag_second: float32 [256, 256], P('col')
The draws below stay inside these ranges and needn't reach their ends.
Inputs may be any that keep to these rules, and one draw needn't show every extreme that they name: `struct_first`: 72 distinct block indices in increasing order; the last is always 96 - 1. `struct_second`: 48 distinct block indices in increasing order, each also listed in struct_first; the last is always 96 - 1; the second supernode's whole structure is the first supernode together with these blocks. `inv_first`: lower triangular with a positive diagonal. `inv_second`: lower triangular with a positive diagonal.
All inputs are finite; a program needn't handle non-finite values.
Results may differ from the reference program's by a relative error of at most 0.0041.
Values may be sent and summed in bfloat16 or wider, within the bound.
A program may use at most 64 MiB of HBM per device.

```python
import math
import jax
import jax.numpy as jnp
from jax import lax

B = 256
CB = 3
NB = 96
RB = 6
P1 = 72
P2 = 48
N_ROW = 16
N_COL = 32


def lower_factor(key):
    first, second = jax.random.split(key)
    row_index = jnp.arange(B)[:, None]
    col_index = jnp.arange(B)[None, :]
    lower_part = jax.random.normal(first, (B, B), jnp.float32) * (0.8 / math.sqrt(B))
    diagonal = jax.random.uniform(second, (B,), jnp.float32, 0.5, 2.0)
    return jnp.where(row_index > col_index, lower_part, 0.0) + jnp.where(row_index == col_index, diagonal[:, None], 0.0)


def draw_inv_first(key, part):
    return lower_factor(jax.random.fold_in(key, 11))


def draw_inv_second(key, part):
    return lower_factor(jax.random.fold_in(key, 12))


def structure(key):
    shuffled = jax.random.permutation(jax.random.fold_in(key, 5), NB - 1).astype(jnp.int32)
    root_block = jnp.full((1,), NB - 1, jnp.int32)
    return (shuffled, root_block)


def draw_struct_first(key, part):
    shuffled, root_block = structure(key)
    return jnp.sort(jnp.concatenate([shuffled[:P1 - 1], root_block]))


def draw_struct_second(key, part):
    shuffled, root_block = structure(key)
    return jnp.sort(jnp.concatenate([shuffled[:P2 - 1], root_block]))


def levels(own_key, dims, shards, least, largest):
    level = 1.0
    for position, blocks in shards:
        draws = jax.random.uniform(jax.random.fold_in(jax.random.fold_in(own_key, 6), position), (blocks,), jnp.float32, least / len(shards), largest / len(shards))
        level = level * jnp.repeat(jnp.exp(draws), dims[position] // blocks).reshape((-1,) + (1,) * (len(dims) - 1 - position))
    return level


def noise(key, dims, deviation, most, cuts=(), kind=jnp.bfloat16):
    values = deviation * jax.random.normal(key, dims, jnp.float32)
    if cuts:
        values = values * levels(key, dims, cuts, -0.22, 0.18)
    return jnp.clip(values, -most, most).astype(kind)


def setup_inputs(seed: int = 0) -> dict:
    splits = jax.random.split(jax.random.key(seed), 9)
    return {
        "stored_inverse": noise(splits[0], (RB, N_ROW, CB, N_COL, B, B), 1.0, 6.0, ((1, 16), (3, 32))),
        "panel_first": noise(splits[1], (RB, N_ROW, B, B), (P1 * B) ** -0.5, 0.046875, ((1, 16), (2, 32))),
        "panel_second": noise(splits[2], (RB, N_ROW, B, B), (P2 * B) ** -0.5, 0.0546875, ((1, 16), (2, 32))),
        "panel_link": noise(splits[3], (B, B), B ** -0.5, 0.375),
        "inv_first": draw_inv_first(jax.random.fold_in(splits[8], 71), 0),
        "inv_second": draw_inv_second(jax.random.fold_in(splits[8], 71), 0),
        "struct_first": draw_struct_first(jax.random.fold_in(splits[8], 71), 0),
        "struct_second": draw_struct_second(jax.random.fold_in(splits[8], 71), 0),
    }


precise = lax.Precision.HIGHEST


def member(struct):
    block_ids = jnp.arange(NB, dtype=jnp.int32)
    return jnp.any(block_ids[:, None] == struct[None, :], axis=1)


def block_products(blocks, factors):
    factors_wide = factors.astype(jnp.float32)

    def one_row(block_row):
        return jnp.einsum("kij,kjl->il", block_row.astype(jnp.float32), factors_wide, precision=precise)

    return lax.map(one_row, blocks)


def factor_blocks(panel, inverse, mask):
    product = jnp.einsum("kij,jl->kil", panel.astype(jnp.float32), inverse, precision=precise)
    return jnp.where(mask[:, None, None], product, 0.0).astype(jnp.bfloat16)


def reference(stored_inverse, panel_first, panel_second, panel_link, inv_first, inv_second, struct_first, struct_second):
    blocks = stored_inverse.reshape(NB, NB, B, B)
    mask_first = member(struct_first)
    mask_second = member(struct_second)
    factor_first = factor_blocks(panel_first.reshape(NB, B, B), inv_first, mask_first)
    column_first = jnp.where(mask_first[:, None, None], -block_products(blocks, factor_first), 0.0)
    diag_first = jnp.dot(inv_first.T, inv_first, precision=precise) - jnp.einsum(
        "kij,kil->jl", factor_first.astype(jnp.float32), column_first, precision=precise)
    factor_second = factor_blocks(panel_second.reshape(NB, B, B), inv_second, mask_second)
    link_wide = jnp.dot(panel_link.astype(jnp.float32), inv_second, precision=precise)
    link_block = -(jnp.einsum("kij,kil->jl", column_first, factor_second.astype(jnp.float32), precision=precise)
                   + jnp.dot(diag_first, link_wide, precision=precise))
    carried = jnp.einsum("kij,jl->kil", column_first, link_wide, precision=precise)
    column_second = jnp.where(mask_second[:, None, None], -(block_products(blocks, factor_second) + carried), 0.0)
    diag_second = (jnp.dot(inv_second.T, inv_second, precision=precise)
                   - jnp.einsum("kij,kil->jl", factor_second.astype(jnp.float32), column_second, precision=precise)
                   - jnp.dot(link_wide.T, link_block, precision=precise))
    return (column_first.reshape(RB, N_ROW, B, B), column_second.reshape(RB, N_ROW, B, B),
            diag_first, link_block, diag_second)
```

```python
import jax
import jax.numpy as jnp
from jax import lax
from jax.experimental import pallas as pl
from jax.experimental.pallas import tpu as pltpu
from jax.sharding import PartitionSpec as P

NX, NY, NZ = 4, 8, 8
F32, BF16 = jnp.float32, jnp.bfloat16
precise = lax.Precision.HIGHEST


def dev(row, col):
    return {"row": row, "col": col}


def fdot(a, b):
    return jnp.dot(a, b, preferred_element_type=F32, precision=precise)


def tdot(a, b):
    return lax.dot_general(a, b, (((0,), (0,)), ((), ())), preferred_element_type=F32, precision=precise)


def wait_bytes(ref, sem):
    pltpu.make_async_copy(ref, ref, sem).wait()


def listed(struct_ref, block):
    hit = jnp.where(struct_ref[...] == block, 1.0, 0.0)
    return jnp.max(hit, axis=1, keepdims=True)


def kernel(
    s_hbm, p1_hbm, p2_hbm, link_hbm, inv1_hbm, inv2_hbm, st1, st2,
    col1, col2, diag1, link, diag2,
    s_v, p_v, link_v, inv_v, wide, gram1, gram2, raw, fac, own_fac,
    half_out, half_in, pair_out, pair_in, kept, z_out, z_in,
    ea_out, ea_in, ea_z, ea_zin, ea_y, ea_yin,
    eb_out, eb_in, eb_z, eb_zin, eb_y, eb_yin, rest, carry,
    load_sem, a_send, send_sem, recv_sem,
):
    row, col = lax.axis_index("row"), lax.axis_index("col")
    y, core = lax.div(row, 2), lax.rem(row, 2)
    z, x = lax.div(col, NX), lax.rem(col, NX)
    quad = lax.rem(y, 4)
    panels = (p1_hbm, p2_hbm)

    loads = [
        pltpu.make_async_copy(p1_hbm, p_v.at[0], load_sem.at[0]),
        pltpu.make_async_copy(p2_hbm, p_v.at[1], load_sem.at[1]),
        pltpu.make_async_copy(inv1_hbm, inv_v.at[0], load_sem.at[2]),
        pltpu.make_async_copy(inv2_hbm, inv_v.at[1], load_sem.at[3]),
        pltpu.make_async_copy(link_hbm, link_v, load_sem.at[4]),
        pltpu.make_async_copy(s_hbm, s_v, load_sem.at[5]),
    ]
    for load in loads:
        load.start()

    barrier = pltpu.get_barrier_semaphore()

    def greet(r, c):
        pl.semaphore_signal(barrier, inc=1, device_id=dev(r, c), device_id_type=pl.DeviceIdType.MESH)

    src_row = lax.rem(col, 16)
    for slot in range(4):
        src_col = 4 * (2 * quad + core) + slot
        me = jnp.logical_and(src_row == row, src_col == col)

        @pl.when(jnp.logical_not(me))
        def _():
            greet(src_row, src_col)

    for d in range(1, NX):
        greet(row, 4 * z + lax.rem(x + d, NX))
    for d in range(1, NZ):
        greet(row, 4 * lax.rem(z + d, NZ) + x)
    for d in range(0, NY):
        for k in range(0, 2):
            if d or k:
                greet(2 * lax.rem(y + d, NY) + lax.rem(core + k, 2), col)

    targets = []
    others = 3 + 7 + 15
    for zhi in range(2):
        for k in range(2):
            r_t = 2 * (lax.div(z, 2) + 4 * k) + lax.rem(z, 2)
            c_t = row + 16 * zhi
            me = jnp.logical_and(r_t == row, c_t == col)
            others = others + jnp.where(me, 0, 1)
            targets.append((zhi, k, r_t, c_t, me))
    pl.semaphore_wait(barrier, others)

    def stage_a(sn, zhi, k, r_t, c_t):
        spot = raw.at[sn, :, lax.div(col, 8), lax.rem(lax.div(col, 4), 2), lax.rem(col, 4)]
        return (
            pltpu.make_async_remote_copy(
                panels[sn].at[:, zhi], spot, a_send.at[sn, 2 * zhi + k], recv_sem.at[0, sn],
                device_id=dev(r_t, c_t), device_id_type=pl.DeviceIdType.MESH),
            pltpu.make_async_copy(panels[sn].at[:, zhi], spot, recv_sem.at[0, sn]),
        )

    for sn in range(2):
        for zhi, k, r_t, c_t, me in targets:
            far, near = stage_a(sn, zhi, k, r_t, c_t)

            @pl.when(jnp.logical_not(me))
            def _():
                far.start()

            @pl.when(me)
            def _():
                near.start()

    for load in loads[:5]:
        load.wait()
    for sn in range(2):
        product = fdot(p_v[sn].astype(F32).reshape(48, 256), inv_v[sn])
        own_fac[sn] = product
    for block in range(6):
        number = block * 16 + row
        m1, m2 = listed(st1, number), listed(st2, number)
        own_fac[0, 8 * block:8 * block + 8, :] = (own_fac[0, 8 * block:8 * block + 8, :] * m1).astype(BF16).astype(F32)
        own_fac[1, 8 * block:8 * block + 8, :] = (own_fac[1, 8 * block:8 * block + 8, :] * m2).astype(BF16).astype(F32)
    wide[...] = fdot(link_v[...].astype(F32), inv_v[1])
    gram1[...] = tdot(inv_v[0], inv_v[0])

    def remote(src, dst, stage, sn, r, c):
        copy = pltpu.make_async_remote_copy(
            src, dst, send_sem.at[stage, sn], recv_sem.at[stage, sn],
            device_id=dev(r, c), device_id_type=pl.DeviceIdType.MESH)
        copy.start()

    for sn in range(2):
        wait_bytes(raw.at[sn, :, quad, core], recv_sem.at[0, sn])
        spot = raw.at[sn, :, quad, core]
        for d in (2, 1, 7):
            remote(spot, spot, 1, sn, 2 * lax.rem(y + d, NY) + core, col)
    gram2[...] = tdot(inv_v[1], inv_v[1]) + tdot(wide[...], fdot(gram1[...], wide[...]))
    for sn in range(2):
        wait_bytes(raw.at[sn, :, pl.ds(0, 3), core], recv_sem.at[1, sn])
        spot = raw.at[sn, :, :, core]
        remote(spot, spot, 2, sn, 2 * y + 1 - core, col)
    loads[5].wait()

    x1 = x + 1 - 2 * lax.rem(x, 2)
    x3 = 3 - x
    rel = (x, x1, lax.rem(x + 2, 4), x3)
    first_peer = (x1, x3)
    second_peer = (x3, x1)
    structs = (st1, st2)

    for sn in range(2):
        wait_bytes(raw.at[sn, :, :, core], recv_sem.at[2, sn])
        upper = inv_v[sn].astype(BF16)
        lower = (inv_v[sn] - upper.astype(F32)).astype(BF16)
        for b in range(3):
            rows = raw[sn, b].astype(F32).reshape(256, 256).astype(BF16)
            product = jnp.dot(rows, upper, preferred_element_type=F32) + jnp.dot(rows, lower, preferred_element_type=F32)
            fac[sn, b] = (product * listed(structs[sn], b * 32 + col)).astype(BF16)
        for half in range(2):
            def block_row(step, _):
                a = 3 * half + step
                total = jnp.dot(s_v[a, 0], fac[sn, 0], preferred_element_type=F32)
                total += jnp.dot(s_v[a, 1], fac[sn, 1], preferred_element_type=F32)
                total += jnp.dot(s_v[a, 2], fac[sn, 2], preferred_element_type=F32)
                for xd in range(NX):
                    slot = lax.rem(rel[xd] + 3, 4) if half == 0 else 3 - rel[xd]
                    for zd in range(NZ):
                        at = 8 * (4 * zd + xd)
                        half_out[sn, half, slot, zd, step] = total[at:at + 8, :].astype(BF16)
                return 0

            lax.fori_loop(0, 3, block_row, 0)
            remote(half_out.at[sn, half, pl.ds(0, 2)], half_in.at[sn, half], 3 + half, sn, row, 4 * z + first_peer[half])

    for sn in range(2):
        for half in range(2):
            wait_bytes(half_in.at[sn, half], recv_sem.at[3 + half, sn])
            pair_out[sn, half] = (half_out[sn, half, 2].astype(F32) + half_in[sn, half, 1].astype(F32)).astype(BF16)
            remote(pair_out.at[sn, half], pair_in.at[sn, half], 5 + half, sn, row, 4 * z + second_peer[half])
            kept[half] = half_out[sn, half, 3].astype(F32) + half_in[sn, half, 0].astype(F32)
        for half in range(2):
            wait_bytes(pair_in.at[sn, half], recv_sem.at[5 + half, sn])
            z_out[sn, :, 3 * half:3 * half + 3] = (kept[half] + pair_in[sn, half].astype(F32)).astype(BF16)
        for d in (4, 3, 5, 2, 6, 1, 7):
            to = lax.rem(z + d, NZ)
            remote(z_out.at[sn, to], z_in.at[sn, d - 1], 7, sn, row, 4 * to + x)

    def z_total(sn):
        wait_bytes(z_in.at[sn], recv_sem.at[7, sn])
        total = z_out[sn, z].astype(F32)
        for d in range(7):
            total += z_in[sn, d].astype(F32)
        return total

    total = z_total(0)
    for block in range(6):
        col1[block] = total[block] * (-listed(st1, block * 16 + row))
    first = tdot(own_fac[0], col1[...].reshape(48, 256))
    top = tdot(col1[...].reshape(48, 256), own_fac[1])

    def spread_rows(out, m, matrix):
        for xd in range(NX):
            for zd in range(NZ):
                at = 8 * (4 * zd + xd)
                out[xd, zd, m] = matrix[at:at + 8, :].astype(BF16)

    spread_rows(ea_out, 0, first)
    spread_rows(ea_out, 1, top)
    for d in (2, 1, 3):
        to = lax.rem(x + d, NX)
        remote(ea_out.at[to], ea_in.at[d - 1], 8, 0, row, 4 * z + to)
    rest[...] = tdot(wide[...], fdot(first, wide[...]) - top)
    carry[...] = fdot(col1[...].reshape(48, 256), wide[...])

    total = z_total(1).reshape(48, 256) + carry[...]
    for block in range(6):
        col2[block] = total[8 * block:8 * block + 8, :] * (-listed(st2, block * 16 + row))
    second = tdot(own_fac[1], col2[...].reshape(48, 256)) + rest[...]
    spread_rows(eb_out, 0, second)
    for d in (2, 1, 3):
        to = lax.rem(x + d, NX)
        remote(eb_out.at[to], eb_in.at[d - 1], 8, 1, row, 4 * z + to)

    groups = ((ea_out, ea_in, ea_z, ea_zin, ea_y, ea_yin), (eb_out, eb_in, eb_z, eb_zin, eb_y, eb_yin))
    for g, (g_out, g_in, g_z, g_zin, g_y, g_yin) in enumerate(groups):
        wait_bytes(g_in, recv_sem.at[8, g])
        total = g_out[x].astype(F32)
        for d in range(3):
            total += g_in[d].astype(F32)
        g_z[...] = total.astype(BF16)
        for d in (4, 3, 5, 2, 6, 1, 7):
            to = lax.rem(z + d, NZ)
            remote(g_z.at[to], g_zin.at[d - 1], 9, g, row, 4 * to + x)
    for g, (g_out, g_in, g_z, g_zin, g_y, g_yin) in enumerate(groups):
        wait_bytes(g_zin, recv_sem.at[9, g])
        total = g_z[z].astype(F32)
        for d in range(7):
            total += g_zin[d].astype(F32)
        g_y[...] = total
        for d in (4, 3, 5, 2, 6, 1, 7, 0):
            for k in range(2):
                if d or k:
                    to = 2 * lax.rem(y + d, NY) + lax.rem(core + k, 2)
                    remote(g_y, g_yin.at[2 * d + k - 1], 10, g, to, col)

    def y_total(g):
        g_y, g_yin = groups[g][4:]
        wait_bytes(g_yin, recv_sem.at[10, g])
        total = g_y[...]
        for d in range(15):
            total += g_yin[d]
        return total

    at = pl.multiple_of(8 * col, 8)
    total = y_total(0)
    diag1[...] = gram1[pl.ds(at, 8), :] - total[0]
    link[...] = -(total[1] + fdot(diag1[...], wide[...]))
    diag2[...] = gram2[pl.ds(at, 8), :] - y_total(1)[0]

    for sn in range(2):
        for zhi, k, r_t, c_t, me in targets:
            far, _ = stage_a(sn, zhi, k, r_t, c_t)

            @pl.when(jnp.logical_not(me))
            def _():
                far.wait_send()

        wait_bytes(raw.at[sn, :, pl.ds(0, 3), core], send_sem.at[1, sn])
        wait_bytes(raw.at[sn, :, :, core], send_sem.at[2, sn])
        for half in range(2):
            wait_bytes(half_in.at[sn, half], send_sem.at[3 + half, sn])
            wait_bytes(pair_in.at[sn, half], send_sem.at[5 + half, sn])
        wait_bytes(z_in.at[sn], send_sem.at[7, sn])
        wait_bytes(groups[sn][1], send_sem.at[8, sn])
        wait_bytes(groups[sn][3], send_sem.at[9, sn])
        wait_bytes(groups[sn][5], send_sem.at[10, sn])


def body(stored_inverse, panel_first, panel_second, panel_link, inv_first, inv_second, struct_first, struct_second):
    anywhere = pl.BlockSpec(memory_space=pl.ANY)
    vmem = pl.BlockSpec(memory_space=pltpu.VMEM)

    def e_scratch(n):
        return [
            pltpu.VMEM((4, 8, n, 8, 256), BF16), pltpu.VMEM((3, 8, n, 8, 256), BF16),
            pltpu.VMEM((8, n, 8, 256), BF16), pltpu.VMEM((7, n, 8, 256), BF16),
            pltpu.VMEM((n, 8, 256), F32), pltpu.VMEM((15, n, 8, 256), F32),
        ]

    c1, c2, d1, lk, d2 = pl.pallas_call(
        kernel,
        out_shape=[jax.ShapeDtypeStruct((6, 8, 256), F32)] * 2 + [jax.ShapeDtypeStruct((8, 256), F32)] * 3,
        in_specs=[anywhere] * 6 + [vmem] * 2,
        out_specs=[vmem] * 5,
        scratch_shapes=[
            pltpu.VMEM((6, 3, 256, 256), BF16),
            pltpu.VMEM((2, 3, 2, 8, 256), BF16),
            pltpu.VMEM((256, 256), BF16),
            pltpu.VMEM((2, 256, 256), F32),
            pltpu.VMEM((256, 256), F32),
            pltpu.VMEM((256, 256), F32),
            pltpu.VMEM((256, 256), F32),
            pltpu.VMEM((2, 3, 4, 2, 4, 8, 256), BF16),
            pltpu.VMEM((2, 3, 256, 256), BF16),
            pltpu.VMEM((2, 48, 256), F32),
            pltpu.VMEM((2, 2, 4, 8, 3, 8, 256), BF16),
            pltpu.VMEM((2, 2, 2, 8, 3, 8, 256), BF16),
            pltpu.VMEM((2, 2, 8, 3, 8, 256), BF16),
            pltpu.VMEM((2, 2, 8, 3, 8, 256), BF16),
            pltpu.VMEM((2, 8, 3, 8, 256), F32),
            pltpu.VMEM((2, 8, 6, 8, 256), BF16),
            pltpu.VMEM((2, 7, 6, 8, 256), BF16),
            *e_scratch(2),
            *e_scratch(1),
            pltpu.VMEM((256, 256), F32),
            pltpu.VMEM((48, 256), F32),
            pltpu.SemaphoreType.DMA((6,)),
            pltpu.SemaphoreType.DMA((2, 4)),
            pltpu.SemaphoreType.DMA((11, 2)),
            pltpu.SemaphoreType.DMA((11, 2)),
        ],
        compiler_params=pltpu.CompilerParams(
            collective_id=0, has_side_effects=True, vmem_limit_bytes=40 * 1024 * 1024),
    )(
        stored_inverse.reshape(6, 3, 256, 256),
        panel_first.reshape(3, 2, 8, 256),
        panel_second.reshape(3, 2, 8, 256),
        panel_link, inv_first, inv_second,
        struct_first.reshape(1, -1), struct_second.reshape(1, -1),
    )
    return c1.reshape(6, 1, 8, 256), c2.reshape(6, 1, 8, 256), d1, lk, d2


def solution(mesh):
    return jax.shard_map(
        body,
        mesh=mesh,
        in_specs=(P(None, "row", None, "col", None, None), P(None, "row", "col", None), P(None, "row", "col", None),
                  P(), P(), P(), P(), P()),
        out_specs=(P(None, "row", "col", None), P(None, "row", "col", None), P("col", None), P("col", None), P("col", None)),
        check_vma=False,
    )
```

```python
import jax
import jax.numpy as jnp
from jax import lax
from jax.experimental import pallas as pl
from jax.experimental.pallas import tpu as pltpu
from jax.sharding import PartitionSpec as P

NX, NY, NZ = 4, 8, 8
F32, BF16 = jnp.float32, jnp.bfloat16
precise = lax.Precision.HIGHEST


def dev(row, col):
    return {"row": row, "col": col}


def fdot(a, b):
    return jnp.dot(a, b, preferred_element_type=F32, precision=precise)


def tdot(a, b):
    return lax.dot_general(a, b, (((0,), (0,)), ((), ())), preferred_element_type=F32, precision=precise)


def wait_bytes(ref, sem):
    pltpu.make_async_copy(ref, ref, sem).wait()


def listed(struct_ref, block):
    hit = jnp.where(struct_ref[...] == block, 1.0, 0.0)
    return jnp.max(hit, axis=1, keepdims=True)


def kernel(
    s_hbm, p1_hbm, p2_hbm, link_hbm, inv1_hbm, inv2_hbm, st1_hbm, st2_hbm,
    out,
    st1, st2, s_v, link_v, inv_v, wide, tall, gram1, gram2, rows_z, masked, fac_t, raw, fac,
    part_out, part_in, summed, z_out, z_in,
    ea_own, ea_twin, ea_out, ea_in, ea_z, ea_zin, ea_y, ea_yin, ea_sum,
    eb_own, eb_twin, eb_out, eb_in, eb_z, eb_zin, eb_y, eb_yin, eb_sum, rest, carry,
    load_sem, a_send, send_sem, recv_sem,
):
    row, col = lax.axis_index("row"), lax.axis_index("col")
    col1, col2 = out.at[pl.ds(0, 6)], out.at[pl.ds(6, 6)]
    diag1, link, diag2 = out.at[12], out.at[13], out.at[14]
    y, core = lax.div(row, 2), lax.rem(row, 2)
    z, x = lax.div(col, NX), lax.rem(col, NX)
    quad = lax.rem(y, 4)

    loads = [
        pltpu.make_async_copy(p1_hbm, rows_z.at[z, 0], load_sem.at[0]),
        pltpu.make_async_copy(p2_hbm, rows_z.at[z, 1], load_sem.at[1]),
        pltpu.make_async_copy(inv1_hbm, inv_v.at[0], load_sem.at[2]),
        pltpu.make_async_copy(inv2_hbm, inv_v.at[1], load_sem.at[3]),
        pltpu.make_async_copy(link_hbm, link_v, load_sem.at[4]),
        pltpu.make_async_copy(st1_hbm, st1, load_sem.at[6]),
        pltpu.make_async_copy(st2_hbm, st2, load_sem.at[7]),
        pltpu.make_async_copy(s_hbm, s_v, load_sem.at[5]),
    ]
    for load in loads:
        load.start()

    barrier = pltpu.get_barrier_semaphore()

    def greet(r, c):
        pl.semaphore_signal(barrier, inc=1, device_id=dev(r, c), device_id_type=pl.DeviceIdType.MESH)

    src_row = lax.rem(col, 16)
    for slot in range(4):
        src_col = 4 * (2 * quad + core) + slot
        me = jnp.logical_and(src_row == row, src_col == col)

        @pl.when(jnp.logical_not(me))
        def _():
            greet(src_row, src_col)

    for d in range(1, NZ):
        greet(row, 4 * lax.rem(z + d, NZ) + x)
    for d in range(1, NX):
        greet(row, 4 * z + lax.rem(x + d, NX))
    for d in range(1, NY):
        greet(2 * lax.rem(y + d, NY) + core, col)
    twin = 2 * y + 1 - core
    greet(twin, col)

    targets = []
    others = 3 + 7 + 7 + 1
    for zhi in range(2):
        for k in range(2):
            r_t = 2 * (lax.div(z, 2) + 4 * k) + lax.rem(z, 2)
            c_t = row + 16 * zhi
            me = jnp.logical_and(r_t == row, c_t == col)
            others = others + jnp.where(me, 0, 1)
            targets.append((zhi, k, r_t, c_t, me))
    loads[0].wait()
    loads[1].wait()
    pl.semaphore_wait(barrier, others)

    spot_a = raw.at[:, :, lax.div(col, 8), lax.rem(lax.div(col, 4), 2), lax.rem(col, 4)]

    def stage_a(zhi, k, r_t, c_t):
        return pltpu.make_async_remote_copy(
            rows_z.at[z, :, :, zhi], spot_a, a_send.at[2 * zhi + k], recv_sem.at[0, 0],
            device_id=dev(r_t, c_t), device_id_type=pl.DeviceIdType.MESH)

    for zhi, k, r_t, c_t, me in targets:
        @pl.when(jnp.logical_not(me))
        def _():
            stage_a(zhi, k, r_t, c_t).start()

        @pl.when(me)
        def _():
            pltpu.make_async_copy(rows_z.at[z, :, :, zhi], spot_a, recv_sem.at[0, 0]).start()

    def remote(src, dst, stage, sn, r, c):
        pltpu.make_async_remote_copy(
            src, dst, send_sem.at[stage, sn], recv_sem.at[stage, sn],
            device_id=dev(r, c), device_id_type=pl.DeviceIdType.MESH).start()

    wait_bytes(raw.at[:, :, quad, core], recv_sem.at[0, 0])
    for sn in range(2):
        spot = raw.at[sn, :, quad, core]
        for d in (2 + 4 * sn, 1, 7):
            remote(spot, spot, 1, sn, 2 * lax.rem(y + d, NY) + core, col)
    for d in (4, 3, 5, 2, 6, 1, 7):
        remote(rows_z.at[z], rows_z.at[z], 5, 0, row, 4 * lax.rem(z + d, NZ) + x)
    for load in loads[2:-1]:
        load.wait()
    wide[...] = fdot(link_v[...].astype(F32), inv_v[1])
    for sn in range(2):
        wait_bytes(raw.at[sn, :, pl.ds(0, 3), core], recv_sem.at[1, sn])
        spot = raw.at[sn, :, :, core]
        remote(spot, spot, 2, sn, twin, col)
    loads[-1].wait()

    structs = (st1, st2)
    uppers = [inv_v[sn].astype(BF16) for sn in range(2)]
    lowers = [(inv_v[sn] - uppers[sn].astype(F32)).astype(BF16) for sn in range(2)]

    def times_inverse(rows, sn):
        return (jnp.dot(rows, uppers[sn], preferred_element_type=F32)
                + jnp.dot(rows, lowers[sn], preferred_element_type=F32))

    for sn in range(2):
        wait_bytes(raw.at[sn, :, :, core], recv_sem.at[2, sn])
        for b in range(3):
            rows = raw[sn, b].astype(F32).reshape(256, 256).astype(BF16)
            fac[sn, b] = (times_inverse(rows, sn) * listed(structs[sn], b * 32 + col)).astype(BF16)
        for half in range(2):
            def block_row(step, _):
                a = 3 * half + step
                total = jnp.dot(s_v[a, 0], fac[sn, 0], preferred_element_type=F32)
                total += jnp.dot(s_v[a, 1], fac[sn, 1], preferred_element_type=F32)
                total += jnp.dot(s_v[a, 2], fac[sn, 2], preferred_element_type=F32)
                for xd in range(NX):
                    for zd in range(NZ):
                        at = 8 * (4 * zd + xd)
                        part_out[sn, half, xd, zd, step] = total[at:at + 8, :].astype(BF16)
                return 0

            lax.fori_loop(0, 3, block_row, 0)
            for d in (2, 1, 3):
                to = lax.rem(x + d, NX)
                remote(part_out.at[sn, half, to], part_in.at[sn, half, d - 1], 3 + half, sn, row, 4 * z + to)

    wait_bytes(rows_z.at[pl.ds(0, 7)], recv_sem.at[5, 0])
    for sn in range(2):
        for block in range(6):
            masked[:, block] = rows_z[:, sn, block // 2, block % 2].astype(F32) * listed(structs[sn], block * 16 + row)
        product = times_inverse(masked[...].reshape(384, 256).astype(BF16), sn)
        fac_t[sn] = product.T.astype(BF16)
    tall[...] = wide[...].T

    def spread_rows(to, m, matrix):
        for xd in range(NX):
            for zd in range(NZ):
                at = 8 * (4 * zd + xd)
                for lanes in range(2):
                    to[lanes, xd, zd, m] = matrix[at:at + 8, 128 * lanes:128 * lanes + 128]

    groups = ((ea_own, ea_twin, ea_out, ea_in, ea_z, ea_zin, ea_y, ea_yin, ea_sum),
              (eb_own, eb_twin, eb_out, eb_in, eb_z, eb_zin, eb_y, eb_yin, eb_sum))
    for sn in range(2):
        for half in range(2):
            wait_bytes(part_in.at[sn, half], recv_sem.at[3 + half, sn])
            total = part_out[sn, half, x].astype(F32)
            for d in range(3):
                total += part_in[sn, half, d].astype(F32)
            summed[:, 3 * half:3 * half + 3] = total
            z_out[sn, :, 3 * half:3 * half + 3] = total.astype(BF16)
        for d in (4, 3, 5, 2, 6, 1, 7):
            to = lax.rem(z + d, NZ)
            remote(z_out.at[sn, to], z_in.at[sn, d - 1], 7, sn, row, 4 * to + x)
        high = summed[...].reshape(384, 256).astype(BF16)
        low = (summed[...].reshape(384, 256) - high.astype(F32)).astype(BF16)

        def part_sum(which):
            return -(jnp.dot(fac_t[which], high, preferred_element_type=F32)
                     + jnp.dot(fac_t[which], low, preferred_element_type=F32))

        g_own, g_twin, g_out, g_in = groups[sn][:4]
        if sn == 0:
            first = part_sum(0)
            top_t = part_sum(1)
            top = top_t.T
            spread_rows(g_own, 0, first)
            spread_rows(g_own, 1, top)
        else:
            spread_rows(g_own, 0, part_sum(1) + rest[...])
        remote(g_own.at[1 - core], g_twin, 6, sn, twin, col)
        if sn == 0:
            rest[...] = fdot(tall[...], fdot(first, wide[...]) - top) - fdot(top_t, wide[...])
        wait_bytes(g_twin, recv_sem.at[6, sn])
        g_out[...] = (g_own[core] + g_twin[...]).astype(BF16)
        for d in (2, 1, 3):
            to = lax.rem(x + d, NX)
            remote(g_out.at[to], g_in.at[d - 1], 8, sn, row, 4 * z + to)

    for g in range(2):
        g_out, g_in, g_z, g_zin = groups[g][2:6]
        wait_bytes(g_in, recv_sem.at[8, g])
        total = g_out[x].astype(F32)
        for d in range(3):
            total += g_in[d].astype(F32)
        g_z[...] = total.astype(BF16)
        for d in (4, 3, 5, 2, 6, 1, 7):
            to = lax.rem(z + d, NZ)
            remote(g_z.at[to], g_zin.at[d - 1], 9, g, row, 4 * to + x)
    gram1[...] = tdot(inv_v[0], inv_v[0])
    gram2[...] = tdot(inv_v[1], inv_v[1]) + fdot(tall[...], fdot(gram1[...], wide[...]))

    def z_total(sn):
        wait_bytes(z_in.at[sn], recv_sem.at[7, sn])
        total = z_out[sn, z].astype(F32)
        for d in range(7):
            total += z_in[sn, d].astype(F32)
        return total

    total = z_total(0)
    for block in range(6):
        col1[block] = total[block] * (-listed(st1, block * 16 + row))
    carry[...] = fdot(col1[...].reshape(48, 256), wide[...])

    for g in range(2):
        g_z, g_zin, g_y, g_yin = groups[g][4:8]
        wait_bytes(g_zin, recv_sem.at[9, g])
        total = g_z[z].astype(F32)
        for d in range(7):
            total += g_zin[d].astype(F32)
        g_y[...] = total
        for d in (4, 3, 5, 2, 6, 1, 7):
            remote(g_y, g_yin.at[d - 1], 10, g, 2 * lax.rem(y + d, NY) + core, col)

    total = z_total(1).reshape(48, 256) + carry[...]
    for block in range(6):
        col2[block] = total[8 * block:8 * block + 8, :] * (-listed(st2, block * 16 + row))

    for g in range(2):
        g_y, g_yin, g_sum = groups[g][6:9]
        wait_bytes(g_yin, recv_sem.at[10, g])
        total = g_y[...]
        for d in range(7):
            total += g_yin[d]
        g_sum[core] = total
        remote(g_sum.at[core], g_sum.at[core], 11, g, twin, col)
    for g in range(2):
        wait_bytes(groups[g][8].at[core], recv_sem.at[11, g])

    at = pl.multiple_of(8 * col, 8)

    def whole(g_sum, m):
        return jnp.concatenate([g_sum[0, m], g_sum[1, m]], axis=1)

    diag1[...] = gram1[pl.ds(at, 8), :] - whole(ea_sum, 0)
    link[...] = -(whole(ea_sum, 1) + fdot(diag1[...], wide[...]))
    diag2[...] = gram2[pl.ds(at, 8), :] - whole(eb_sum, 0)

    for zhi, k, r_t, c_t, me in targets:
        @pl.when(jnp.logical_not(me))
        def _():
            stage_a(zhi, k, r_t, c_t).wait_send()

    wait_bytes(rows_z.at[pl.ds(0, 7)], send_sem.at[5, 0])
    for sn in range(2):
        wait_bytes(raw.at[sn, :, pl.ds(0, 3), core], send_sem.at[1, sn])
        wait_bytes(raw.at[sn, :, :, core], send_sem.at[2, sn])
        for half in range(2):
            wait_bytes(part_in.at[sn, half], send_sem.at[3 + half, sn])
        wait_bytes(z_in.at[sn], send_sem.at[7, sn])
        wait_bytes(groups[sn][1], send_sem.at[6, sn])
        wait_bytes(groups[sn][3], send_sem.at[8, sn])
        wait_bytes(groups[sn][5], send_sem.at[9, sn])
        wait_bytes(groups[sn][7], send_sem.at[10, sn])
        wait_bytes(groups[sn][8].at[core], send_sem.at[11, sn])


def body(stored_inverse, panel_first, panel_second, panel_link, inv_first, inv_second, struct_first, struct_second):
    anywhere = pl.BlockSpec(memory_space=pl.ANY)
    vmem = pl.BlockSpec(memory_space=pltpu.VMEM)

    def e_scratch(n):
        return [
            pltpu.VMEM((2, 4, 8, n, 8, 128), F32), pltpu.VMEM((4, 8, n, 8, 128), F32),
            pltpu.VMEM((4, 8, n, 8, 128), BF16), pltpu.VMEM((3, 8, n, 8, 128), BF16),
            pltpu.VMEM((8, n, 8, 128), BF16), pltpu.VMEM((7, n, 8, 128), BF16),
            pltpu.VMEM((n, 8, 128), F32), pltpu.VMEM((7, n, 8, 128), F32), pltpu.VMEM((2, n, 8, 128), F32),
        ]

    out = pl.pallas_call(
        kernel,
        out_shape=jax.ShapeDtypeStruct((15, 8, 256), F32),
        in_specs=[anywhere] * 8,
        out_specs=vmem,
        scratch_shapes=[
            pltpu.VMEM(struct_first.reshape(1, -1).shape, jnp.int32),
            pltpu.VMEM(struct_second.reshape(1, -1).shape, jnp.int32),
            pltpu.VMEM((6, 3, 256, 256), BF16),
            pltpu.VMEM((256, 256), BF16),
            pltpu.VMEM((2, 256, 256), F32),
            pltpu.VMEM((256, 256), F32),
            pltpu.VMEM((256, 256), F32),
            pltpu.VMEM((256, 256), F32),
            pltpu.VMEM((256, 256), F32),
            pltpu.VMEM((8, 2, 3, 2, 8, 256), BF16),
            pltpu.VMEM((8, 6, 8, 256), F32),
            pltpu.VMEM((2, 256, 384), BF16),
            pltpu.VMEM((2, 3, 4, 2, 4, 8, 256), BF16),
            pltpu.VMEM((2, 3, 256, 256), BF16),
            pltpu.VMEM((2, 2, 4, 8, 3, 8, 256), BF16),
            pltpu.VMEM((2, 2, 3, 8, 3, 8, 256), BF16),
            pltpu.VMEM((8, 6, 8, 256), F32),
            pltpu.VMEM((2, 8, 6, 8, 256), BF16),
            pltpu.VMEM((2, 7, 6, 8, 256), BF16),
            *e_scratch(2),
            *e_scratch(1),
            pltpu.VMEM((256, 256), F32),
            pltpu.VMEM((48, 256), F32),
            pltpu.SemaphoreType.DMA((8,)),
            pltpu.SemaphoreType.DMA((4,)),
            pltpu.SemaphoreType.DMA((12, 2)),
            pltpu.SemaphoreType.DMA((12, 2)),
        ],
        compiler_params=pltpu.CompilerParams(
            collective_id=0, has_side_effects=True, vmem_limit_bytes=40 * 1024 * 1024),
    )(
        *[pltpu.with_memory_space_constraint(v, pltpu.HBM) for v in (
            stored_inverse.reshape(6, 3, 256, 256),
            panel_first.reshape(3, 2, 8, 256),
            panel_second.reshape(3, 2, 8, 256),
            panel_link, inv_first, inv_second,
            struct_first.reshape(1, -1), struct_second.reshape(1, -1),
        )])
    c1, c2, d1, lk, d2 = out[:6], out[6:12], out[12], out[13], out[14]
    return c1.reshape(6, 1, 8, 256), c2.reshape(6, 1, 8, 256), d1, lk, d2


def solution(mesh):
    return jax.shard_map(
        body,
        mesh=mesh,
        in_specs=(P(None, "row", None, "col", None, None), P(None, "row", "col", None), P(None, "row", "col", None),
                  P(), P(), P(), P(), P()),
        out_specs=(P(None, "row", "col", None), P(None, "row", "col", None), P("col", None), P("col", None), P("col", None)),
        check_vma=False,
    )
```

```python
import jax
import jax.numpy as jnp
from jax import lax
from jax.experimental import pallas as pl
from jax.experimental.pallas import tpu as pltpu
from jax.sharding import PartitionSpec as P

NX, NY, NZ = 4, 8, 8
F32, BF16 = jnp.float32, jnp.bfloat16
precise = lax.Precision.HIGHEST


def dev(row, col):
    return {"row": row, "col": col}


def fdot(a, b):
    return jnp.dot(a, b, preferred_element_type=F32, precision=precise)


def tdot(a, b):
    return lax.dot_general(a, b, (((0,), (0,)), ((), ())), preferred_element_type=F32, precision=precise)


def wait_bytes(ref, sem):
    pltpu.make_async_copy(ref, ref, sem).wait()


def listed(struct_ref, block):
    hit = jnp.where(struct_ref[...] == block, 1.0, 0.0)
    return jnp.max(hit, axis=1, keepdims=True)


def kernel(
    s_hbm, p1_hbm, p2_hbm, link_hbm, inv1_hbm, inv2_hbm, st1_hbm, st2_hbm,
    out,
    st1, st2, s_v, link_v, inv_v, wide, tall, gram1, gram2, p_v, rows_z, rows_x, ordered, fac_t, raw, fac,
    q_out, q_in, q_x, q_xin, part_out, part_in, summed, z_out, z_in,
    ea_own, ea_twin, ea_out, ea_in, ea_z, ea_zin, ea_y, ea_yin, ea_sum,
    eb_own, eb_twin, eb_out, eb_in, eb_z, eb_zin, eb_y, eb_yin, eb_sum, rest, carry,
    load_sem, a_send, send_sem, recv_sem,
):
    row, col = lax.axis_index("row"), lax.axis_index("col")
    col1, col2 = out.at[pl.ds(0, 6)], out.at[pl.ds(6, 6)]
    diag1, link, diag2 = out.at[12], out.at[13], out.at[14]
    y, core = lax.div(row, 2), lax.rem(row, 2)
    z, x = lax.div(col, NX), lax.rem(col, NX)
    quad = lax.rem(y, 4)

    loads = [
        pltpu.make_async_copy(p1_hbm, p_v.at[0], load_sem.at[0]),
        pltpu.make_async_copy(p2_hbm, p_v.at[1], load_sem.at[1]),
        pltpu.make_async_copy(inv1_hbm, inv_v.at[0], load_sem.at[2]),
        pltpu.make_async_copy(inv2_hbm, inv_v.at[1], load_sem.at[3]),
        pltpu.make_async_copy(link_hbm, link_v, load_sem.at[4]),
        pltpu.make_async_copy(st1_hbm, st1, load_sem.at[6]),
        pltpu.make_async_copy(st2_hbm, st2, load_sem.at[7]),
        pltpu.make_async_copy(s_hbm, s_v, load_sem.at[5]),
    ]
    for load in loads:
        load.start()

    barrier = pltpu.get_barrier_semaphore()

    def greet(r, c):
        pl.semaphore_signal(barrier, inc=1, device_id=dev(r, c), device_id_type=pl.DeviceIdType.MESH)

    src_row = lax.rem(col, 16)
    for slot in range(4):
        src_col = 4 * (2 * quad + core) + slot
        me = jnp.logical_and(src_row == row, src_col == col)

        @pl.when(jnp.logical_not(me))
        def _():
            greet(src_row, src_col)

    for d in range(1, NZ):
        greet(row, 4 * lax.rem(z + d, NZ) + x)
    for d in range(1, NX):
        greet(row, 4 * z + lax.rem(x + d, NX))
    for d in range(1, NY):
        greet(2 * lax.rem(y + d, NY) + core, col)
    twin = 2 * y + 1 - core
    greet(twin, col)

    targets = []
    others = 3 + 7 + 7 + 1
    for zhi in range(2):
        for k in range(2):
            r_t = 2 * (lax.div(z, 2) + 4 * k) + lax.rem(z, 2)
            c_t = row + 16 * zhi
            me = jnp.logical_and(r_t == row, c_t == col)
            others = others + jnp.where(me, 0, 1)
            targets.append((zhi, k, r_t, c_t, me))
    for load in loads[:-1]:
        load.wait()
    structs = (st1, st2)
    uppers = [inv_v[sn].astype(BF16) for sn in range(2)]
    for sn in range(2):
        lower = (inv_v[sn] - uppers[sn].astype(F32)).astype(BF16)
        rows = jnp.concatenate([
            p_v[sn, block // 2, block % 2].astype(F32) * listed(structs[sn], block * 16 + row) for block in range(6)
        ], axis=0).astype(BF16)
        product = (jnp.dot(rows, uppers[sn], preferred_element_type=F32)
                   + jnp.dot(rows, lower, preferred_element_type=F32))
        rows_z[z, sn] = product.reshape(3, 2, 8, 256).astype(BF16)
    rows_x[x] = rows_z[z, 1]
    pl.semaphore_wait(barrier, others)

    spot_a = raw.at[:, :, lax.div(col, 8), lax.rem(lax.div(col, 4), 2), lax.rem(col, 4)]

    def stage_a(zhi, k, r_t, c_t):
        return pltpu.make_async_remote_copy(
            rows_z.at[z, :, :, zhi], spot_a, a_send.at[2 * zhi + k], recv_sem.at[0, 0],
            device_id=dev(r_t, c_t), device_id_type=pl.DeviceIdType.MESH)

    for zhi, k, r_t, c_t, me in targets:
        @pl.when(jnp.logical_not(me))
        def _():
            stage_a(zhi, k, r_t, c_t).start()

        @pl.when(me)
        def _():
            pltpu.make_async_copy(rows_z.at[z, :, :, zhi], spot_a, recv_sem.at[0, 0]).start()

    def remote(src, dst, stage, sn, r, c):
        pltpu.make_async_remote_copy(
            src, dst, send_sem.at[stage, sn], recv_sem.at[stage, sn],
            device_id=dev(r, c), device_id_type=pl.DeviceIdType.MESH).start()

    wait_bytes(raw.at[:, :, quad, core], recv_sem.at[0, 0])
    for sn in range(2):
        spot = raw.at[sn, :, quad, core]
        for d in (2 + 4 * sn, 1, 7):
            remote(spot, spot, 1, sn, 2 * lax.rem(y + d, NY) + core, col)
    for d in (4, 3, 5, 2, 6, 1, 7):
        remote(rows_z.at[z], rows_z.at[z], 5, 0, row, 4 * lax.rem(z + d, NZ) + x)
    for d in (2, 1, 3):
        remote(rows_x.at[x], rows_x.at[x], 14, 0, row, 4 * z + lax.rem(x + d, NX))
    wide[...] = fdot(link_v[...].astype(F32), inv_v[1])
    for sn in range(2):
        wait_bytes(raw.at[sn, :, pl.ds(0, 3), core], recv_sem.at[1, sn])
        spot = raw.at[sn, :, :, core]
        remote(spot, spot, 2, sn, twin, col)
    loads[-1].wait()

    for sn in range(2):
        wait_bytes(raw.at[sn, :, :, core], recv_sem.at[2, sn])
        for b in range(3):
            fac[sn, b] = raw[sn, b].astype(F32).reshape(256, 256).astype(BF16)
        for half in ((0, 1) if sn == 0 else (1, 0)):
            def block_row(step, _):
                a = 3 * half + step
                total = jnp.dot(s_v[a, 0], fac[sn, 0], preferred_element_type=F32)
                total += jnp.dot(s_v[a, 1], fac[sn, 1], preferred_element_type=F32)
                total += jnp.dot(s_v[a, 2], fac[sn, 2], preferred_element_type=F32)
                for xd in range(NX):
                    for zd in range(NZ):
                        at = 8 * (4 * zd + xd)
                        piece = total[at:at + 8, :].astype(BF16)
                        if sn and half:
                            q_out[zd, xd, step] = piece
                        else:
                            part_out[2 * sn + half, xd, zd, step] = piece
                return 0

            lax.fori_loop(0, 3, block_row, 0)
            if sn and half:
                for d in (4, 3, 5, 2, 6, 1, 7):
                    to = lax.rem(z + d, NZ)
                    remote(q_out.at[to], q_in.at[d - 1], 12, 0, row, 4 * to + x)
            else:
                n = 2 * sn + half
                for d in (2, 1, 3):
                    to = lax.rem(x + d, NX)
                    remote(part_out.at[n, to], part_in.at[n, d - 1], 3 + half, sn, row, 4 * z + to)

    wait_bytes(rows_z.at[pl.ds(0, 7)], recv_sem.at[5, 0])
    wait_bytes(rows_x.at[pl.ds(0, 3)], recv_sem.at[14, 0])
    for sn in range(2):
        for block in range(6):
            ordered[block // 3, :, block % 3] = rows_z[:, sn, block // 2, block % 2].astype(F32)
        fac_t[sn] = ordered[...].reshape(384, 256).T.astype(BF16)
    tall[...] = wide[...].T

    def spread_rows(to, m, matrix):
        for xd in range(NX):
            for zd in range(NZ):
                at = 8 * (4 * zd + xd)
                for lanes in range(2):
                    to[lanes, xd, zd, m] = matrix[at:at + 8, 128 * lanes:128 * lanes + 128]

    groups = ((ea_own, ea_twin, ea_out, ea_in, ea_z, ea_zin, ea_y, ea_yin, ea_sum),
              (eb_own, eb_twin, eb_out, eb_in, eb_z, eb_zin, eb_y, eb_yin, eb_sum))
    for sn in range(2):
        for half in range(2 - sn):
            n = 2 * sn + half
            wait_bytes(part_in.at[n], recv_sem.at[3 + half, sn])
            total = part_out[n, x].astype(F32)
            for d in range(3):
                total += part_in[n, d].astype(F32)
            summed[half] = total
            z_out[n] = total.astype(BF16)
            for d in (4, 3, 5, 2, 6, 1, 7):
                to = lax.rem(z + d, NZ)
                remote(z_out.at[n, to], z_in.at[n, d - 1], 7 + 8 * half, sn, row, 4 * to + x)
        depth = 384 - 192 * sn
        sums = (summed[...] if sn == 0 else summed[0]).reshape(depth, 256)
        high = sums.astype(BF16)
        low = (sums - high.astype(F32)).astype(BF16)

        def part_sum(which):
            factor = fac_t[which, :, 0:depth]
            return -(jnp.dot(factor, high, preferred_element_type=F32)
                     + jnp.dot(factor, low, preferred_element_type=F32))

        g_own, g_twin, g_out, g_in = groups[sn][:4]
        if sn == 0:
            first = part_sum(0)
            top_t = part_sum(1)
            top = top_t.T
            spread_rows(g_own, 0, first)
            spread_rows(g_own, 1, top)
        else:
            second = part_sum(1) + rest[...]
            wait_bytes(q_in, recv_sem.at[12, 0])
            total = q_out[z].astype(F32)
            for d in range(7):
                total += q_in[d].astype(F32)
            q_x[...] = total.astype(BF16)
            for d in (2, 1, 3):
                to = lax.rem(x + d, NX)
                remote(q_x.at[to], q_xin.at[d - 1], 13, 0, row, 4 * z + to)
            late = jnp.stack([rows_x[:, block // 2, block % 2].astype(F32) for block in (3, 4, 5)], axis=1)
            spread_rows(g_own, 0, second - tdot(late.reshape(96, 256), total.reshape(96, 256)))
        remote(g_own.at[1 - core], g_twin, 6, sn, twin, col)
        if sn == 0:
            rest[...] = fdot(tall[...], fdot(first, wide[...]) - top) - fdot(top_t, wide[...])
        wait_bytes(g_twin, recv_sem.at[6, sn])
        g_out[...] = (g_own[core] + g_twin[...]).astype(BF16)
        for d in (2, 1, 3):
            to = lax.rem(x + d, NX)
            remote(g_out.at[to], g_in.at[d - 1], 8, sn, row, 4 * z + to)

    for g in range(2):
        g_out, g_in, g_z, g_zin = groups[g][2:6]
        wait_bytes(g_in, recv_sem.at[8, g])
        total = g_out[x].astype(F32)
        for d in range(3):
            total += g_in[d].astype(F32)
        g_z[...] = total.astype(BF16)
        for d in (4, 3, 5, 2, 6, 1, 7):
            to = lax.rem(z + d, NZ)
            remote(g_z.at[to], g_zin.at[d - 1], 9, g, row, 4 * to + x)
    gram1[...] = tdot(inv_v[0], inv_v[0])
    gram2[...] = tdot(inv_v[1], inv_v[1]) + fdot(tall[...], fdot(gram1[...], wide[...]))

    def z_total(n, stage, sn):
        wait_bytes(z_in.at[n], recv_sem.at[stage, sn])
        total = z_out[n, z].astype(F32)
        for d in range(7):
            total += z_in[n, d].astype(F32)
        return total

    for half in range(2):
        total = z_total(half, 7 + 8 * half, 0)
        for step in range(3):
            block = 3 * half + step
            col1[block] = total[step] * (-listed(st1, block * 16 + row))
    carry[...] = fdot(col1[...].reshape(48, 256), wide[...])

    for g in range(2):
        g_z, g_zin, g_y, g_yin = groups[g][4:8]
        wait_bytes(g_zin, recv_sem.at[9, g])
        total = g_z[z].astype(F32)
        for d in range(7):
            total += g_zin[d].astype(F32)
        g_y[...] = total
        for d in (4, 3, 5, 2, 6, 1, 7):
            remote(g_y, g_yin.at[d - 1], 10, g, 2 * lax.rem(y + d, NY) + core, col)

    early = z_total(2, 7, 1)
    wait_bytes(q_xin, recv_sem.at[13, 0])
    late = q_x[x].astype(F32)
    for d in range(3):
        late += q_xin[d].astype(F32)
    for block in range(6):
        total = (early if block < 3 else late)[block % 3] + carry[8 * block:8 * block + 8, :]
        col2[block] = total * (-listed(st2, block * 16 + row))

    for g in range(2):
        g_y, g_yin, g_sum = groups[g][6:9]
        wait_bytes(g_yin, recv_sem.at[10, g])
        total = g_y[...]
        for d in range(7):
            total += g_yin[d]
        g_sum[core] = total
        remote(g_sum.at[core], g_sum.at[core], 11, g, twin, col)
    for g in range(2):
        wait_bytes(groups[g][8].at[core], recv_sem.at[11, g])

    at = pl.multiple_of(8 * col, 8)

    def whole(g_sum, m):
        return jnp.concatenate([g_sum[0, m], g_sum[1, m]], axis=1)

    diag1[...] = gram1[pl.ds(at, 8), :] - whole(ea_sum, 0)
    link[...] = -(whole(ea_sum, 1) + fdot(diag1[...], wide[...]))
    diag2[...] = gram2[pl.ds(at, 8), :] - whole(eb_sum, 0)

    for zhi, k, r_t, c_t, me in targets:
        @pl.when(jnp.logical_not(me))
        def _():
            stage_a(zhi, k, r_t, c_t).wait_send()

    wait_bytes(rows_z.at[pl.ds(0, 7)], send_sem.at[5, 0])
    wait_bytes(rows_x.at[pl.ds(0, 3)], send_sem.at[14, 0])
    wait_bytes(q_in, send_sem.at[12, 0])
    wait_bytes(q_xin, send_sem.at[13, 0])
    for sn in range(2):
        wait_bytes(raw.at[sn, :, pl.ds(0, 3), core], send_sem.at[1, sn])
        wait_bytes(raw.at[sn, :, :, core], send_sem.at[2, sn])
        for half in range(2 - sn):
            wait_bytes(part_in.at[2 * sn + half], send_sem.at[3 + half, sn])
            wait_bytes(z_in.at[2 * sn + half], send_sem.at[7 + 8 * half, sn])
        wait_bytes(groups[sn][1], send_sem.at[6, sn])
        wait_bytes(groups[sn][3], send_sem.at[8, sn])
        wait_bytes(groups[sn][5], send_sem.at[9, sn])
        wait_bytes(groups[sn][7], send_sem.at[10, sn])
        wait_bytes(groups[sn][8].at[core], send_sem.at[11, sn])


def body(stored_inverse, panel_first, panel_second, panel_link, inv_first, inv_second, struct_first, struct_second):
    anywhere = pl.BlockSpec(memory_space=pl.ANY)
    vmem = pl.BlockSpec(memory_space=pltpu.VMEM)

    def e_scratch(n):
        return [
            pltpu.VMEM((2, 4, 8, n, 8, 128), F32), pltpu.VMEM((4, 8, n, 8, 128), F32),
            pltpu.VMEM((4, 8, n, 8, 128), BF16), pltpu.VMEM((3, 8, n, 8, 128), BF16),
            pltpu.VMEM((8, n, 8, 128), BF16), pltpu.VMEM((7, n, 8, 128), BF16),
            pltpu.VMEM((n, 8, 128), F32), pltpu.VMEM((7, n, 8, 128), F32), pltpu.VMEM((2, n, 8, 128), F32),
        ]

    out = pl.pallas_call(
        kernel,
        out_shape=jax.ShapeDtypeStruct((15, 8, 256), F32),
        in_specs=[anywhere] * 8,
        out_specs=vmem,
        scratch_shapes=[
            pltpu.VMEM(struct_first.reshape(1, -1).shape, jnp.int32),
            pltpu.VMEM(struct_second.reshape(1, -1).shape, jnp.int32),
            pltpu.VMEM((6, 3, 256, 256), BF16),
            pltpu.VMEM((256, 256), BF16),
            pltpu.VMEM((2, 256, 256), F32),
            pltpu.VMEM((256, 256), F32),
            pltpu.VMEM((256, 256), F32),
            pltpu.VMEM((256, 256), F32),
            pltpu.VMEM((256, 256), F32),
            pltpu.VMEM((2, 3, 2, 8, 256), BF16),
            pltpu.VMEM((8, 2, 3, 2, 8, 256), BF16),
            pltpu.VMEM((4, 3, 2, 8, 256), BF16),
            pltpu.VMEM((2, 8, 3, 8, 256), F32),
            pltpu.VMEM((2, 256, 384), BF16),
            pltpu.VMEM((2, 3, 4, 2, 4, 8, 256), BF16),
            pltpu.VMEM((2, 3, 256, 256), BF16),
            pltpu.VMEM((8, 4, 3, 8, 256), BF16),
            pltpu.VMEM((7, 4, 3, 8, 256), BF16),
            pltpu.VMEM((4, 3, 8, 256), BF16),
            pltpu.VMEM((3, 3, 8, 256), BF16),
            pltpu.VMEM((3, 4, 8, 3, 8, 256), BF16),
            pltpu.VMEM((3, 3, 8, 3, 8, 256), BF16),
            pltpu.VMEM((2, 8, 3, 8, 256), F32),
            pltpu.VMEM((3, 8, 3, 8, 256), BF16),
            pltpu.VMEM((3, 7, 3, 8, 256), BF16),
            *e_scratch(2),
            *e_scratch(1),
            pltpu.VMEM((256, 256), F32),
            pltpu.VMEM((48, 256), F32),
            pltpu.SemaphoreType.DMA((8,)),
            pltpu.SemaphoreType.DMA((4,)),
            pltpu.SemaphoreType.DMA((16, 2)),
            pltpu.SemaphoreType.DMA((16, 2)),
        ],
        compiler_params=pltpu.CompilerParams(
            collective_id=0, has_side_effects=True, vmem_limit_bytes=40 * 1024 * 1024),
    )(
        *[pltpu.with_memory_space_constraint(v, pltpu.HBM) for v in (
            stored_inverse.reshape(6, 3, 256, 256),
            panel_first.reshape(3, 2, 8, 256),
            panel_second.reshape(3, 2, 8, 256),
            panel_link, inv_first, inv_second,
            struct_first.reshape(1, -1), struct_second.reshape(1, -1),
        )])
    c1, c2, d1, lk, d2 = out[:6], out[6:12], out[12], out[13], out[14]
    return c1.reshape(6, 1, 8, 256), c2.reshape(6, 1, 8, 256), d1, lk, d2


def solution(mesh):
    return jax.shard_map(
        body,
        mesh=mesh,
        in_specs=(P(None, "row", None, "col", None, None), P(None, "row", "col", None), P(None, "row", "col", None),
                  P(), P(), P(), P(), P()),
        out_specs=(P(None, "row", "col", None), P(None, "row", "col", None), P("col", None), P("col", None), P("col", None)),
        check_vma=False,
    )
```

```python
import jax
import jax.numpy as jnp
from jax import lax
from jax.experimental import pallas as pl
from jax.experimental.pallas import tpu as pltpu
from jax.sharding import PartitionSpec as P

NX, NY, NZ = 4, 8, 8
F32, BF16 = jnp.float32, jnp.bfloat16
precise = lax.Precision.HIGHEST


def dev(row, col):
    return {"row": row, "col": col}


def fdot(a, b):
    return jnp.dot(a, b, preferred_element_type=F32, precision=precise)


def tdot(a, b):
    return lax.dot_general(a, b, (((0,), (0,)), ((), ())), preferred_element_type=F32, precision=precise)


def wait_bytes(ref, sem):
    pltpu.make_async_copy(ref, ref, sem).wait()


def listed(struct_ref, block):
    hit = jnp.where(struct_ref[...] == block, 1.0, 0.0)
    return jnp.max(hit, axis=1, keepdims=True)


def kernel(
    s_hbm, p1_hbm, p2_hbm, link_hbm, inv1_hbm, inv2_hbm, st1_hbm, st2_hbm,
    out,
    st1, st2, s_v, link_v, inv_v, wide, tall, gram1, gram2, p_v, rows_z, rows_x, ordered, fac_t, raw, fac,
    q_out, q_in, q_x, q_xin, part_out, part_in, summed, z_out, z_in,
    ea_own, ea_twin, ea_out, ea_in, ea_z, ea_zin, ea_y, ea_yin, ea_sum,
    eb_own, eb_twin, eb_out, eb_in, eb_z, eb_zin, eb_y, eb_yin, eb_sum, rest, carry,
    load_sem, a_send, send_sem, recv_sem,
):
    row, col = lax.axis_index("row"), lax.axis_index("col")
    col1, col2 = out.at[pl.ds(0, 6)], out.at[pl.ds(6, 6)]
    diag1, link, diag2 = out.at[12], out.at[13], out.at[14]
    y, core = lax.div(row, 2), lax.rem(row, 2)
    z, x = lax.div(col, NX), lax.rem(col, NX)
    part = lax.rem(lax.rem(z, 4) + 2 + lax.div(lax.rem(col, 16), 2) + 4 - lax.rem(y, 4), 4)

    loads = [
        pltpu.make_async_copy(p1_hbm, p_v.at[0], load_sem.at[0]),
        pltpu.make_async_copy(p2_hbm, p_v.at[1], load_sem.at[1]),
        pltpu.make_async_copy(inv1_hbm, inv_v.at[0], load_sem.at[2]),
        pltpu.make_async_copy(inv2_hbm, inv_v.at[1], load_sem.at[3]),
        pltpu.make_async_copy(link_hbm, link_v, load_sem.at[4]),
        pltpu.make_async_copy(st1_hbm, st1, load_sem.at[6]),
        pltpu.make_async_copy(st2_hbm, st2, load_sem.at[7]),
        pltpu.make_async_copy(s_hbm, s_v, load_sem.at[5]),
    ]
    for load in loads:
        load.start()

    barrier = pltpu.get_barrier_semaphore()

    def greet(r, c):
        pl.semaphore_signal(barrier, inc=1, device_id=dev(r, c), device_id_type=pl.DeviceIdType.MESH)

    src_row = lax.rem(col, 16)
    for slot in range(4):
        src_col = 4 * (4 * core + part) + slot
        me = jnp.logical_and(src_row == row, src_col == col)

        @pl.when(jnp.logical_not(me))
        def _():
            greet(src_row, src_col)

    for d in range(1, NZ):
        greet(row, 4 * lax.rem(z + d, NZ) + x)
    for d in range(1, NX):
        greet(row, 4 * z + lax.rem(x + d, NX))
    for d in range(1, NY):
        greet(2 * lax.rem(y + d, NY) + core, col)
    twin = 2 * y + 1 - core
    greet(twin, col)

    targets = []
    others = 3 + 7 + 7 + 1
    for zhi in range(2):
        for k in range(2):
            r_t = 2 * (lax.rem(y + 10 - z + lax.div(row, 4), 4) + 4 * k) + lax.div(z, 4)
            c_t = row + 16 * zhi
            me = jnp.logical_and(r_t == row, c_t == col)
            others = others + jnp.where(me, 0, 1)
            targets.append((zhi, k, r_t, c_t, me))
    for load in loads[:-1]:
        load.wait()
    structs = (st1, st2)
    uppers = [inv_v[sn].astype(BF16) for sn in range(2)]
    for sn in range(2):
        lower = (inv_v[sn] - uppers[sn].astype(F32)).astype(BF16)
        rows = jnp.concatenate([
            p_v[sn, block // 2, block % 2].astype(F32) * listed(structs[sn], block * 16 + row) for block in range(6)
        ], axis=0).astype(BF16)
        product = (jnp.dot(rows, uppers[sn], preferred_element_type=F32)
                   + jnp.dot(rows, lower, preferred_element_type=F32))
        rows_z[z, sn] = product.reshape(3, 2, 8, 256).astype(BF16)
    rows_x[x] = rows_z[z, 1]
    pl.semaphore_wait(barrier, others)

    spot_a = raw.at[:, :, lax.div(z, 4), lax.rem(z, 4), x]

    def stage_a(zhi, k, r_t, c_t):
        return pltpu.make_async_remote_copy(
            rows_z.at[z, :, :, zhi], spot_a, a_send.at[2 * zhi + k], recv_sem.at[0, 0],
            device_id=dev(r_t, c_t), device_id_type=pl.DeviceIdType.MESH)

    for zhi, k, r_t, c_t, me in targets:
        @pl.when(jnp.logical_not(me))
        def _():
            stage_a(zhi, k, r_t, c_t).start()

        @pl.when(me)
        def _():
            pltpu.make_async_copy(rows_z.at[z, :, :, zhi], spot_a, recv_sem.at[0, 0]).start()

    def remote(src, dst, stage, sn, r, c):
        pltpu.make_async_remote_copy(
            src, dst, send_sem.at[stage, sn], recv_sem.at[stage, sn],
            device_id=dev(r, c), device_id_type=pl.DeviceIdType.MESH).start()

    wait_bytes(raw.at[:, :, core, part], recv_sem.at[0, 0])
    for sn in range(2):
        spot = raw.at[sn, :, core, part]
        for d in (2 + 4 * sn, 1, 7):
            remote(spot, spot, 1, sn, 2 * lax.rem(y + d, NY) + core, col)
    for d in (4, 3, 5, 2, 6, 1, 7):
        remote(rows_z.at[z], rows_z.at[z], 5, 0, row, 4 * lax.rem(z + d, NZ) + x)
    for d in (2, 1, 3):
        remote(rows_x.at[x], rows_x.at[x], 14, 0, row, 4 * z + lax.rem(x + d, NX))
    wide[...] = fdot(link_v[...].astype(F32), inv_v[1])
    for sn in range(2):
        wait_bytes(raw.at[sn, :, core, pl.ds(0, 3)], recv_sem.at[1, sn])
        spot = raw.at[sn, :, core]
        remote(spot, spot, 2, sn, twin, col)
    loads[-1].wait()

    for sn in range(2):
        wait_bytes(raw.at[sn, :, core], recv_sem.at[2, sn])
        for b in range(3):
            fac[sn, b] = raw[sn, b].astype(F32).reshape(256, 256).astype(BF16)
        for half in ((0, 1) if sn == 0 else (1, 0)):
            def block_row(step, _):
                a = 3 * half + step
                total = jnp.dot(s_v[a, 0], fac[sn, 0], preferred_element_type=F32)
                total += jnp.dot(s_v[a, 1], fac[sn, 1], preferred_element_type=F32)
                total += jnp.dot(s_v[a, 2], fac[sn, 2], preferred_element_type=F32)
                for xd in range(NX):
                    for zd in range(NZ):
                        at = 8 * (4 * zd + xd)
                        piece = total[at:at + 8, :].astype(BF16)
                        if sn and half:
                            q_out[zd, xd, step] = piece
                        else:
                            part_out[2 * sn + half, xd, zd, step] = piece
                return 0

            lax.fori_loop(0, 3, block_row, 0)
            if sn and half:
                for d in (4, 3, 5, 2, 6, 1, 7):
                    to = lax.rem(z + d, NZ)
                    remote(q_out.at[to], q_in.at[d - 1], 12, 0, row, 4 * to + x)
            else:
                n = 2 * sn + half
                for d in (2, 1, 3):
                    to = lax.rem(x + d, NX)
                    remote(part_out.at[n, to], part_in.at[n, d - 1], 3 + half, sn, row, 4 * z + to)

    wait_bytes(rows_z.at[pl.ds(0, 7)], recv_sem.at[5, 0])
    wait_bytes(rows_x.at[pl.ds(0, 3)], recv_sem.at[14, 0])
    for sn in range(2):
        for block in range(6):
            ordered[block // 3, :, block % 3] = rows_z[:, sn, block // 2, block % 2].astype(F32)
        fac_t[sn] = ordered[...].reshape(384, 256).T.astype(BF16)
    tall[...] = wide[...].T

    def spread_rows(to, m, matrix):
        for xd in range(NX):
            for zd in range(NZ):
                at = 8 * (4 * zd + xd)
                for lanes in range(2):
                    to[lanes, xd, zd, m] = matrix[at:at + 8, 128 * lanes:128 * lanes + 128]

    groups = ((ea_own, ea_twin, ea_out, ea_in, ea_z, ea_zin, ea_y, ea_yin, ea_sum),
              (eb_own, eb_twin, eb_out, eb_in, eb_z, eb_zin, eb_y, eb_yin, eb_sum))

    def send_z(n, half, sn):
        for d in (4, 3, 5, 2, 6, 1, 7):
            to = lax.rem(z + d, NZ)
            remote(z_out.at[n, to], z_in.at[n, d - 1], 7 + 8 * half, sn, row, 4 * to + x)

    def sum_x(g):
        g_out, g_in, g_z, g_zin = groups[g][2:6]
        wait_bytes(g_in, recv_sem.at[8, g])
        total = g_out[x].astype(F32)
        for d in range(3):
            total += g_in[d].astype(F32)
        g_z[...] = total.astype(BF16)
        for d in (4, 3, 5, 2, 6, 1, 7):
            to = lax.rem(z + d, NZ)
            remote(g_z.at[to], g_zin.at[d - 1], 9, g, row, 4 * to + x)

    def sum_z(g):
        g_z, g_zin, g_y, g_yin = groups[g][4:8]
        wait_bytes(g_zin, recv_sem.at[9, g])
        total = g_z[z].astype(F32)
        for d in range(7):
            total += g_zin[d].astype(F32)
        g_y[...] = total
        for d in (4, 3, 5, 2, 6, 1, 7):
            remote(g_y, g_yin.at[d - 1], 10, g, 2 * lax.rem(y + d, NY) + core, col)

    for sn in range(2):
        for half in range(2 - sn):
            n = 2 * sn + half
            wait_bytes(part_in.at[n], recv_sem.at[3 + half, sn])
            total = part_out[n, x].astype(F32)
            for d in range(3):
                total += part_in[n, d].astype(F32)
            summed[half] = total
            z_out[n] = total.astype(BF16)
            if sn == 0:
                send_z(n, half, sn)
        depth = 384 - 192 * sn
        sums = (summed[...] if sn == 0 else summed[0]).reshape(depth, 256)
        high = sums.astype(BF16)
        low = (sums - high.astype(F32)).astype(BF16)

        def part_sum(which):
            factor = fac_t[which, :, 0:depth]
            return -(jnp.dot(factor, high, preferred_element_type=F32)
                     + jnp.dot(factor, low, preferred_element_type=F32))

        g_own, g_twin, g_out, g_in = groups[sn][:4]
        if sn == 0:
            first = part_sum(0)
            top_t = part_sum(1)
            top = top_t.T
            spread_rows(g_own, 0, first)
            spread_rows(g_own, 1, top)
        else:
            second = part_sum(1) + rest[...]
            wait_bytes(q_in, recv_sem.at[12, 0])
            total = q_out[z].astype(F32)
            for d in range(7):
                total += q_in[d].astype(F32)
            q_x[...] = total.astype(BF16)
            late = jnp.stack([rows_x[:, block // 2, block % 2].astype(F32) for block in (3, 4, 5)], axis=1)
            spread_rows(g_own, 0, second - tdot(late.reshape(96, 256), total.reshape(96, 256)))
        remote(g_own.at[1 - core], g_twin, 6, sn, twin, col)
        if sn:
            send_z(2, 0, 1)
            for d in (2, 1, 3):
                to = lax.rem(x + d, NX)
                remote(q_x.at[to], q_xin.at[d - 1], 13, 0, row, 4 * z + to)
        if sn == 0:
            rest[...] = fdot(tall[...], fdot(first, wide[...]) - top) - fdot(top_t, wide[...])
        wait_bytes(g_twin, recv_sem.at[6, sn])
        g_out[...] = (g_own[core] + g_twin[...]).astype(BF16)
        for d in (2, 1, 3):
            to = lax.rem(x + d, NX)
            remote(g_out.at[to], g_in.at[d - 1], 8, sn, row, 4 * z + to)

    sum_x(0)
    gram1[...] = tdot(inv_v[0], inv_v[0])
    gram2[...] = tdot(inv_v[1], inv_v[1]) + fdot(tall[...], fdot(gram1[...], wide[...]))
    sum_x(1)
    sum_z(0)

    def z_total(n, stage, sn):
        wait_bytes(z_in.at[n], recv_sem.at[stage, sn])
        total = z_out[n, z].astype(F32)
        for d in range(7):
            total += z_in[n, d].astype(F32)
        return total

    for half in range(2):
        total = z_total(half, 7 + 8 * half, 0)
        for step in range(3):
            block = 3 * half + step
            col1[block] = total[step] * (-listed(st1, block * 16 + row))
    carry[...] = fdot(col1[...].reshape(48, 256), wide[...])
    sum_z(1)

    early = z_total(2, 7, 1)
    wait_bytes(q_xin, recv_sem.at[13, 0])
    late = q_x[x].astype(F32)
    for d in range(3):
        late += q_xin[d].astype(F32)
    for block in range(6):
        total = (early if block < 3 else late)[block % 3] + carry[8 * block:8 * block + 8, :]
        col2[block] = total * (-listed(st2, block * 16 + row))

    at = pl.multiple_of(8 * col, 8)

    def whole(g, m):
        g_sum = groups[g][8]
        return jnp.concatenate([g_sum[0, m], g_sum[1, m]], axis=1)

    def sum_y(g):
        g_y, g_yin, g_sum = groups[g][6:9]
        wait_bytes(g_yin, recv_sem.at[10, g])
        total = g_y[...]
        for d in range(7):
            total += g_yin[d]
        g_sum[core] = total
        remote(g_sum.at[core], g_sum.at[core], 11, g, twin, col)

    sum_y(0)
    wait_bytes(ea_sum.at[core], recv_sem.at[11, 0])
    diag1[...] = gram1[pl.ds(at, 8), :] - whole(0, 0)
    link[...] = -(whole(0, 1) + fdot(diag1[...], wide[...]))
    sum_y(1)
    wait_bytes(eb_sum.at[core], recv_sem.at[11, 1])
    diag2[...] = gram2[pl.ds(at, 8), :] - whole(1, 0)

    for zhi, k, r_t, c_t, me in targets:
        @pl.when(jnp.logical_not(me))
        def _():
            stage_a(zhi, k, r_t, c_t).wait_send()

    wait_bytes(rows_z.at[pl.ds(0, 7)], send_sem.at[5, 0])
    wait_bytes(rows_x.at[pl.ds(0, 3)], send_sem.at[14, 0])
    wait_bytes(q_in, send_sem.at[12, 0])
    wait_bytes(q_xin, send_sem.at[13, 0])
    for sn in range(2):
        wait_bytes(raw.at[sn, :, core, pl.ds(0, 3)], send_sem.at[1, sn])
        wait_bytes(raw.at[sn, :, core], send_sem.at[2, sn])
        for half in range(2 - sn):
            wait_bytes(part_in.at[2 * sn + half], send_sem.at[3 + half, sn])
            wait_bytes(z_in.at[2 * sn + half], send_sem.at[7 + 8 * half, sn])
        wait_bytes(groups[sn][1], send_sem.at[6, sn])
        wait_bytes(groups[sn][3], send_sem.at[8, sn])
        wait_bytes(groups[sn][5], send_sem.at[9, sn])
        wait_bytes(groups[sn][7], send_sem.at[10, sn])
        wait_bytes(groups[sn][8].at[core], send_sem.at[11, sn])


def body(stored_inverse, panel_first, panel_second, panel_link, inv_first, inv_second, struct_first, struct_second):
    anywhere = pl.BlockSpec(memory_space=pl.ANY)
    vmem = pl.BlockSpec(memory_space=pltpu.VMEM)

    def e_scratch(n):
        return [
            pltpu.VMEM((2, 4, 8, n, 8, 128), F32), pltpu.VMEM((4, 8, n, 8, 128), F32),
            pltpu.VMEM((4, 8, n, 8, 128), BF16), pltpu.VMEM((3, 8, n, 8, 128), BF16),
            pltpu.VMEM((8, n, 8, 128), BF16), pltpu.VMEM((7, n, 8, 128), BF16),
            pltpu.VMEM((n, 8, 128), F32), pltpu.VMEM((7, n, 8, 128), F32), pltpu.VMEM((2, n, 8, 128), F32),
        ]

    out = pl.pallas_call(
        kernel,
        out_shape=jax.ShapeDtypeStruct((15, 8, 256), F32),
        in_specs=[anywhere] * 8,
        out_specs=vmem,
        scratch_shapes=[
            pltpu.VMEM(struct_first.reshape(1, -1).shape, jnp.int32),
            pltpu.VMEM(struct_second.reshape(1, -1).shape, jnp.int32),
            pltpu.VMEM((6, 3, 256, 256), BF16),
            pltpu.VMEM((256, 256), BF16),
            pltpu.VMEM((2, 256, 256), F32),
            pltpu.VMEM((256, 256), F32),
            pltpu.VMEM((256, 256), F32),
            pltpu.VMEM((256, 256), F32),
            pltpu.VMEM((256, 256), F32),
            pltpu.VMEM((2, 3, 2, 8, 256), BF16),
            pltpu.VMEM((8, 2, 3, 2, 8, 256), BF16),
            pltpu.VMEM((4, 3, 2, 8, 256), BF16),
            pltpu.VMEM((2, 8, 3, 8, 256), F32),
            pltpu.VMEM((2, 256, 384), BF16),
            pltpu.VMEM((2, 3, 2, 4, 4, 8, 256), BF16),
            pltpu.VMEM((2, 3, 256, 256), BF16),
            pltpu.VMEM((8, 4, 3, 8, 256), BF16),
            pltpu.VMEM((7, 4, 3, 8, 256), BF16),
            pltpu.VMEM((4, 3, 8, 256), BF16),
            pltpu.VMEM((3, 3, 8, 256), BF16),
            pltpu.VMEM((3, 4, 8, 3, 8, 256), BF16),
            pltpu.VMEM((3, 3, 8, 3, 8, 256), BF16),
            pltpu.VMEM((2, 8, 3, 8, 256), F32),
            pltpu.VMEM((3, 8, 3, 8, 256), BF16),
            pltpu.VMEM((3, 7, 3, 8, 256), BF16),
            *e_scratch(2),
            *e_scratch(1),
            pltpu.VMEM((256, 256), F32),
            pltpu.VMEM((48, 256), F32),
            pltpu.SemaphoreType.DMA((8,)),
            pltpu.SemaphoreType.DMA((8,)),
            pltpu.SemaphoreType.DMA((16, 2)),
            pltpu.SemaphoreType.DMA((16, 2)),
        ],
        compiler_params=pltpu.CompilerParams(
            collective_id=0, has_side_effects=True, vmem_limit_bytes=40 * 1024 * 1024),
    )(
        *[pltpu.with_memory_space_constraint(v, pltpu.HBM) for v in (
            stored_inverse.reshape(6, 3, 256, 256),
            panel_first.reshape(3, 2, 8, 256),
            panel_second.reshape(3, 2, 8, 256),
            panel_link, inv_first, inv_second,
            struct_first.reshape(1, -1), struct_second.reshape(1, -1),
        )])
    c1, c2, d1, lk, d2 = out[:6], out[6:12], out[12], out[13], out[14]
    return c1.reshape(6, 1, 8, 256), c2.reshape(6, 1, 8, 256), d1, lk, d2


def solution(mesh):
    return jax.shard_map(
        body,
        mesh=mesh,
        in_specs=(P(None, "row", None, "col", None, None), P(None, "row", "col", None), P(None, "row", "col", None),
                  P(), P(), P(), P(), P()),
        out_specs=(P(None, "row", "col", None), P(None, "row", "col", None), P("col", None), P("col", None), P("col", None)),
        check_vma=False,
    )
```

```python
import jax
import jax.numpy as jnp
from jax import lax
from jax.experimental import pallas as pl
from jax.experimental.pallas import tpu as pltpu
from jax.sharding import PartitionSpec as P

NX, NY, NZ = 4, 8, 8
F32, BF16 = jnp.float32, jnp.bfloat16
precise = lax.Precision.HIGHEST


def dev(row, col):
    return {"row": row, "col": col}


def fdot(a, b):
    return jnp.dot(a, b, preferred_element_type=F32, precision=precise)


def tdot(a, b):
    return lax.dot_general(a, b, (((0,), (0,)), ((), ())), preferred_element_type=F32, precision=precise)


def wait_bytes(ref, sem):
    pltpu.make_async_copy(ref, ref, sem).wait()


def listed(struct_ref, block):
    hit = jnp.where(struct_ref[...] == block, 1.0, 0.0)
    return jnp.max(hit, axis=1, keepdims=True)


def kernel(
    s_hbm, p1_hbm, p2_hbm, link_hbm, inv1_hbm, inv2_hbm, st1_hbm, st2_hbm,
    out,
    st1, st2, s_v, link_v, inv_v, wide, tall, gram1, gram2, p_v, rows_z, rows_x, ordered, fac_t, late_t, raw, fac,
    q_out, q_in, q_x, q_xin, part_out, part_in, summed, z_out, z_in,
    ea_own, ea_twin, ea_out, ea_in, ea_z, ea_zin, ea_y, ea_yin, ea_sum,
    eb_own, eb_twin, eb_out, eb_in, eb_z, eb_zin, eb_y, eb_yin, eb_sum, rest, carry,
    load_sem, a_send, send_sem, recv_sem,
):
    row, col = lax.axis_index("row"), lax.axis_index("col")
    col1, col2 = out.at[pl.ds(0, 6)], out.at[pl.ds(6, 6)]
    diag1, link, diag2 = out.at[12], out.at[13], out.at[14]
    y, core = lax.div(row, 2), lax.rem(row, 2)
    z, x = lax.div(col, NX), lax.rem(col, NX)
    part = lax.rem(lax.rem(z, 4) + 2 + lax.div(lax.rem(col, 16), 2) + 4 - lax.rem(y, 4), 4)

    loads = [
        pltpu.make_async_copy(p1_hbm, p_v.at[0], load_sem.at[0]),
        pltpu.make_async_copy(p2_hbm, p_v.at[1], load_sem.at[1]),
        pltpu.make_async_copy(inv1_hbm, inv_v.at[0], load_sem.at[2]),
        pltpu.make_async_copy(inv2_hbm, inv_v.at[1], load_sem.at[3]),
        pltpu.make_async_copy(link_hbm, link_v, load_sem.at[4]),
        pltpu.make_async_copy(st1_hbm, st1, load_sem.at[6]),
        pltpu.make_async_copy(st2_hbm, st2, load_sem.at[7]),
        pltpu.make_async_copy(s_hbm, s_v, load_sem.at[5]),
    ]
    for load in loads:
        load.start()

    barrier = pltpu.get_barrier_semaphore()

    def greet(r, c):
        pl.semaphore_signal(barrier, inc=1, device_id=dev(r, c), device_id_type=pl.DeviceIdType.MESH)

    src_row = lax.rem(col, 16)
    for slot in range(4):
        src_col = 4 * (4 * core + part) + slot
        me = jnp.logical_and(src_row == row, src_col == col)

        @pl.when(jnp.logical_not(me))
        def _():
            greet(src_row, src_col)

    for d in range(1, NZ):
        greet(row, 4 * lax.rem(z + d, NZ) + x)
    for d in range(1, NX):
        greet(row, 4 * z + lax.rem(x + d, NX))
    for d in range(1, NY):
        greet(2 * lax.rem(y + d, NY) + core, col)
    twin = 2 * y + 1 - core
    greet(twin, col)

    targets = []
    others = 3 + 7 + 7 + 1
    for zhi in range(2):
        for k in range(2):
            r_t = 2 * (lax.rem(y + 10 - z + lax.div(row, 4), 4) + 4 * k) + lax.div(z, 4)
            c_t = row + 16 * zhi
            me = jnp.logical_and(r_t == row, c_t == col)
            others = others + jnp.where(me, 0, 1)
            targets.append((zhi, k, r_t, c_t, me))
    for load in loads[:-1]:
        load.wait()
    structs = (st1, st2)
    uppers = [inv_v[sn].astype(BF16) for sn in range(2)]
    for sn in range(2):
        lower = (inv_v[sn] - uppers[sn].astype(F32)).astype(BF16)
        rows = jnp.concatenate([
            p_v[sn, block // 2, block % 2].astype(F32) * listed(structs[sn], block * 16 + row) for block in range(6)
        ], axis=0).astype(BF16)
        product = (jnp.dot(rows, uppers[sn], preferred_element_type=F32)
                   + jnp.dot(rows, lower, preferred_element_type=F32))
        rows_z[z, sn] = product.reshape(3, 2, 8, 256).astype(BF16)
    rows_x[x] = rows_z[z, 1]
    pl.semaphore_wait(barrier, others)

    spot_a = raw.at[:, :, lax.div(z, 4), lax.rem(z, 4), x]

    def stage_a(zhi, k, r_t, c_t):
        return pltpu.make_async_remote_copy(
            rows_z.at[z, :, :, zhi], spot_a, a_send.at[2 * zhi + k], recv_sem.at[0, 0],
            device_id=dev(r_t, c_t), device_id_type=pl.DeviceIdType.MESH)

    for zhi, k, r_t, c_t, me in targets:
        @pl.when(jnp.logical_not(me))
        def _():
            stage_a(zhi, k, r_t, c_t).start()

        @pl.when(me)
        def _():
            pltpu.make_async_copy(rows_z.at[z, :, :, zhi], spot_a, recv_sem.at[0, 0]).start()

    def remote(src, dst, stage, sn, r, c):
        pltpu.make_async_remote_copy(
            src, dst, send_sem.at[stage, sn], recv_sem.at[stage, sn],
            device_id=dev(r, c), device_id_type=pl.DeviceIdType.MESH).start()

    wait_bytes(raw.at[:, :, core, part], recv_sem.at[0, 0])
    for sn in range(2):
        spot = raw.at[sn, :, core, part]
        for d in (2 + 4 * sn, 1, 7):
            remote(spot, spot, 1, sn, 2 * lax.rem(y + d, NY) + core, col)
    for d in (4, 3, 5, 2, 6, 1, 7):
        remote(rows_z.at[z], rows_z.at[z], 5, 0, row, 4 * lax.rem(z + d, NZ) + x)
    for d in (2, 1, 3):
        remote(rows_x.at[x], rows_x.at[x], 14, 0, row, 4 * z + lax.rem(x + d, NX))
    wide[...] = fdot(link_v[...].astype(F32), inv_v[1])
    for sn in range(2):
        wait_bytes(raw.at[sn, :, core, pl.ds(0, 3)], recv_sem.at[1, sn])
        spot = raw.at[sn, :, core]
        remote(spot, spot, 2, sn, twin, col)
    loads[-1].wait()

    for sn in range(2):
        wait_bytes(raw.at[sn, :, core], recv_sem.at[2, sn])
        for b in range(3):
            fac[sn, b] = raw[sn, b].astype(F32).reshape(256, 256).astype(BF16)
        for half in ((0, 1) if sn == 0 else (1, 0)):
            def block_row(step, _):
                a = 3 * half + step
                total = jnp.dot(s_v[a, 0], fac[sn, 0], preferred_element_type=F32)
                total += jnp.dot(s_v[a, 1], fac[sn, 1], preferred_element_type=F32)
                total += jnp.dot(s_v[a, 2], fac[sn, 2], preferred_element_type=F32)
                for xd in range(NX):
                    for zd in range(NZ):
                        at = 8 * (4 * zd + xd)
                        piece = total[at:at + 8, :].astype(BF16)
                        if sn and half:
                            q_out[zd, xd, step] = piece
                        else:
                            part_out[2 * sn + half, xd, zd, step] = piece
                return 0

            lax.fori_loop(0, 3, block_row, 0)
            if sn and half:
                for d in (4, 3, 5, 2, 6, 1, 7):
                    to = lax.rem(z + d, NZ)
                    remote(q_out.at[to], q_in.at[d - 1], 12, 0, row, 4 * to + x)
            else:
                n = 2 * sn + half
                for d in (2, 1, 3):
                    to = lax.rem(x + d, NX)
                    remote(part_out.at[n, to], part_in.at[n, d - 1], 3 + half, sn, row, 4 * z + to)

    wait_bytes(rows_z.at[pl.ds(0, 7)], recv_sem.at[5, 0])
    wait_bytes(rows_x.at[pl.ds(0, 3)], recv_sem.at[14, 0])
    for sn in range(2):
        for block in range(6):
            ordered[block // 3, :, block % 3] = rows_z[:, sn, block // 2, block % 2].astype(F32)
        fac_t[sn] = ordered[...].reshape(384, 256).T.astype(BF16)
    blank = jnp.zeros((32, 256), F32)
    late = jnp.stack([rows_x[:, block // 2, block % 2].astype(F32) for block in (3, 4, 5)], axis=1)
    late_t[...] = jnp.concatenate([late.reshape(96, 256), blank], axis=0).T.astype(BF16)
    tall[...] = wide[...].T
    gram1[...] = tdot(inv_v[0], inv_v[0])
    gram2[...] = tdot(inv_v[1], inv_v[1]) + fdot(tall[...], fdot(gram1[...], wide[...]))

    def spread_rows(to, m, matrix):
        for xd in range(NX):
            for zd in range(NZ):
                at = 8 * (4 * zd + xd)
                for lanes in range(2):
                    to[lanes, xd, zd, m] = matrix[at:at + 8, 128 * lanes:128 * lanes + 128]

    groups = ((ea_own, ea_twin, ea_out, ea_in, ea_z, ea_zin, ea_y, ea_yin, ea_sum),
              (eb_own, eb_twin, eb_out, eb_in, eb_z, eb_zin, eb_y, eb_yin, eb_sum))

    def send_z(n, half, sn):
        for d in (4, 3, 5, 2, 6, 1, 7):
            to = lax.rem(z + d, NZ)
            remote(z_out.at[n, to], z_in.at[n, d - 1], 7 + 8 * half, sn, row, 4 * to + x)

    def sum_x(g):
        g_out, g_in, g_z, g_zin = groups[g][2:6]
        wait_bytes(g_in, recv_sem.at[8, g])
        total = g_out[x].astype(F32)
        for d in range(3):
            total += g_in[d].astype(F32)
        g_z[...] = total.astype(BF16)
        for d in (4, 3, 5, 2, 6, 1, 7):
            to = lax.rem(z + d, NZ)
            remote(g_z.at[to], g_zin.at[d - 1], 9, g, row, 4 * to + x)

    def sum_z(g):
        g_z, g_zin, g_y, g_yin = groups[g][4:8]
        wait_bytes(g_zin, recv_sem.at[9, g])
        total = g_z[z].astype(F32)
        for d in range(7):
            total += g_zin[d].astype(F32)
        g_y[...] = total
        for d in (4, 3, 5, 2, 6, 1, 7):
            remote(g_y, g_yin.at[d - 1], 10, g, 2 * lax.rem(y + d, NY) + core, col)

    for sn in range(2):
        for half in range(2 - sn):
            n = 2 * sn + half
            wait_bytes(part_in.at[n], recv_sem.at[3 + half, sn])
            total = part_out[n, x].astype(F32)
            for d in range(3):
                total += part_in[n, d].astype(F32)
            summed[half] = total
            z_out[n] = total.astype(BF16)
            if sn == 0:
                send_z(n, half, sn)
        depth = 384 - 192 * sn
        sums = (summed[...] if sn == 0 else summed[0]).reshape(depth, 256)
        high = sums.astype(BF16)
        low = (sums - high.astype(F32)).astype(BF16)

        def part_sum(which):
            factor = fac_t[which, :, 0:depth]
            return -(jnp.dot(factor, high, preferred_element_type=F32)
                     + jnp.dot(factor, low, preferred_element_type=F32))

        g_own, g_twin, g_out, g_in = groups[sn][:4]
        if sn == 0:
            first = part_sum(0)
            top_t = part_sum(1)
            top = top_t.T
            spread_rows(g_own, 0, first)
            spread_rows(g_own, 1, top)
        else:
            second = part_sum(1) + rest[...]
            wait_bytes(q_in, recv_sem.at[12, 0])
            total = q_out[z].astype(F32)
            for d in range(7):
                total += q_in[d].astype(F32)
            q_x[...] = total.astype(BF16)
            sums = jnp.concatenate([total.reshape(96, 256), blank], axis=0)
            high = sums.astype(BF16)
            low = (sums - high.astype(F32)).astype(BF16)
            second -= (jnp.dot(late_t[...], high, preferred_element_type=F32)
                       + jnp.dot(late_t[...], low, preferred_element_type=F32))
            spread_rows(g_own, 0, second)
        remote(g_own.at[1 - core], g_twin, 6, sn, twin, col)
        if sn:
            send_z(2, 0, 1)
            for d in (2, 1, 3):
                to = lax.rem(x + d, NX)
                remote(q_x.at[to], q_xin.at[d - 1], 13, 0, row, 4 * z + to)
        if sn == 0:
            rest[...] = fdot(tall[...], fdot(first, wide[...]) - top) - fdot(top_t, wide[...])
        wait_bytes(g_twin, recv_sem.at[6, sn])
        g_out[...] = (g_own[core] + g_twin[...]).astype(BF16)
        for d in (2, 1, 3):
            to = lax.rem(x + d, NX)
            remote(g_out.at[to], g_in.at[d - 1], 8, sn, row, 4 * z + to)

    sum_x(0)
    sum_x(1)
    sum_z(0)

    def z_total(n, stage, sn):
        wait_bytes(z_in.at[n], recv_sem.at[stage, sn])
        total = z_out[n, z].astype(F32)
        for d in range(7):
            total += z_in[n, d].astype(F32)
        return total

    for half in range(2):
        total = z_total(half, 7 + 8 * half, 0)
        for step in range(3):
            block = 3 * half + step
            col1[block] = total[step] * (-listed(st1, block * 16 + row))
    carry[...] = fdot(col1[...].reshape(48, 256), wide[...])
    sum_z(1)

    early = z_total(2, 7, 1)
    wait_bytes(q_xin, recv_sem.at[13, 0])
    late = q_x[x].astype(F32)
    for d in range(3):
        late += q_xin[d].astype(F32)
    for block in range(6):
        total = (early if block < 3 else late)[block % 3] + carry[8 * block:8 * block + 8, :]
        col2[block] = total * (-listed(st2, block * 16 + row))

    at = pl.multiple_of(8 * col, 8)

    def whole(g, m):
        g_sum = groups[g][8]
        return jnp.concatenate([g_sum[0, m], g_sum[1, m]], axis=1)

    def sum_y(g):
        g_y, g_yin, g_sum = groups[g][6:9]
        wait_bytes(g_yin, recv_sem.at[10, g])
        total = g_y[...]
        for d in range(7):
            total += g_yin[d]
        g_sum[core] = total
        remote(g_sum.at[core], g_sum.at[core], 11, g, twin, col)

    for zhi, k, r_t, c_t, me in targets:
        @pl.when(jnp.logical_not(me))
        def _():
            stage_a(zhi, k, r_t, c_t).wait_send()

    wait_bytes(rows_z.at[pl.ds(0, 7)], send_sem.at[5, 0])
    wait_bytes(rows_x.at[pl.ds(0, 3)], send_sem.at[14, 0])
    wait_bytes(q_in, send_sem.at[12, 0])
    wait_bytes(q_xin, send_sem.at[13, 0])
    for sn in range(2):
        wait_bytes(raw.at[sn, :, core, pl.ds(0, 3)], send_sem.at[1, sn])
        wait_bytes(raw.at[sn, :, core], send_sem.at[2, sn])
        for half in range(2 - sn):
            wait_bytes(part_in.at[2 * sn + half], send_sem.at[3 + half, sn])
            wait_bytes(z_in.at[2 * sn + half], send_sem.at[7 + 8 * half, sn])
        wait_bytes(groups[sn][1], send_sem.at[6, sn])
        wait_bytes(groups[sn][3], send_sem.at[8, sn])
        wait_bytes(groups[sn][5], send_sem.at[9, sn])

    sum_y(0)
    wait_bytes(ea_sum.at[core], recv_sem.at[11, 0])
    diag1[...] = gram1[pl.ds(at, 8), :] - whole(0, 0)
    link[...] = -(whole(0, 1) + fdot(diag1[...], wide[...]))
    sum_y(1)
    wait_bytes(eb_sum.at[core], recv_sem.at[11, 1])
    diag2[...] = gram2[pl.ds(at, 8), :] - whole(1, 0)

    for sn in range(2):
        wait_bytes(groups[sn][7], send_sem.at[10, sn])
        wait_bytes(groups[sn][8].at[core], send_sem.at[11, sn])


def body(stored_inverse, panel_first, panel_second, panel_link, inv_first, inv_second, struct_first, struct_second):
    anywhere = pl.BlockSpec(memory_space=pl.ANY)
    vmem = pl.BlockSpec(memory_space=pltpu.VMEM)

    def e_scratch(n):
        return [
            pltpu.VMEM((2, 4, 8, n, 8, 128), F32), pltpu.VMEM((4, 8, n, 8, 128), F32),
            pltpu.VMEM((4, 8, n, 8, 128), BF16), pltpu.VMEM((3, 8, n, 8, 128), BF16),
            pltpu.VMEM((8, n, 8, 128), BF16), pltpu.VMEM((7, n, 8, 128), BF16),
            pltpu.VMEM((n, 8, 128), F32), pltpu.VMEM((7, n, 8, 128), F32), pltpu.VMEM((2, n, 8, 128), F32),
        ]

    out = pl.pallas_call(
        kernel,
        out_shape=jax.ShapeDtypeStruct((15, 8, 256), F32),
        in_specs=[anywhere] * 8,
        out_specs=vmem,
        scratch_shapes=[
            pltpu.VMEM(struct_first.reshape(1, -1).shape, jnp.int32),
            pltpu.VMEM(struct_second.reshape(1, -1).shape, jnp.int32),
            pltpu.VMEM((6, 3, 256, 256), BF16),
            pltpu.VMEM((256, 256), BF16),
            pltpu.VMEM((2, 256, 256), F32),
            pltpu.VMEM((256, 256), F32),
            pltpu.VMEM((256, 256), F32),
            pltpu.VMEM((256, 256), F32),
            pltpu.VMEM((256, 256), F32),
            pltpu.VMEM((2, 3, 2, 8, 256), BF16),
            pltpu.VMEM((8, 2, 3, 2, 8, 256), BF16),
            pltpu.VMEM((4, 3, 2, 8, 256), BF16),
            pltpu.VMEM((2, 8, 3, 8, 256), F32),
            pltpu.VMEM((2, 256, 384), BF16),
            pltpu.VMEM((256, 128), BF16),
            pltpu.VMEM((2, 3, 2, 4, 4, 8, 256), BF16),
            pltpu.VMEM((2, 3, 256, 256), BF16),
            pltpu.VMEM((8, 4, 3, 8, 256), BF16),
            pltpu.VMEM((7, 4, 3, 8, 256), BF16),
            pltpu.VMEM((4, 3, 8, 256), BF16),
            pltpu.VMEM((3, 3, 8, 256), BF16),
            pltpu.VMEM((3, 4, 8, 3, 8, 256), BF16),
            pltpu.VMEM((3, 3, 8, 3, 8, 256), BF16),
            pltpu.VMEM((2, 8, 3, 8, 256), F32),
            pltpu.VMEM((3, 8, 3, 8, 256), BF16),
            pltpu.VMEM((3, 7, 3, 8, 256), BF16),
            *e_scratch(2),
            *e_scratch(1),
            pltpu.VMEM((256, 256), F32),
            pltpu.VMEM((48, 256), F32),
            pltpu.SemaphoreType.DMA((8,)),
            pltpu.SemaphoreType.DMA((8,)),
            pltpu.SemaphoreType.DMA((16, 2)),
            pltpu.SemaphoreType.DMA((16, 2)),
        ],
        compiler_params=pltpu.CompilerParams(
            collective_id=0, has_side_effects=True, vmem_limit_bytes=40 * 1024 * 1024),
    )(
        *[pltpu.with_memory_space_constraint(v, pltpu.HBM) for v in (
            stored_inverse.reshape(6, 3, 256, 256),
            panel_first.reshape(3, 2, 8, 256),
            panel_second.reshape(3, 2, 8, 256),
            panel_link, inv_first, inv_second,
            struct_first.reshape(1, -1), struct_second.reshape(1, -1),
        )])
    c1, c2, d1, lk, d2 = out[:6], out[6:12], out[12], out[13], out[14]
    return c1.reshape(6, 1, 8, 256), c2.reshape(6, 1, 8, 256), d1, lk, d2


def solution(mesh):
    return jax.shard_map(
        body,
        mesh=mesh,
        in_specs=(P(None, "row", None, "col", None, None), P(None, "row", "col", None), P(None, "row", "col", None),
                  P(), P(), P(), P(), P()),
        out_specs=(P(None, "row", "col", None), P(None, "row", "col", None), P("col", None), P("col", None), P("col", None)),
        check_vma=False,
    )
```

```python
import jax
import jax.numpy as jnp
from jax import lax
from jax.experimental import pallas as pl
from jax.experimental.pallas import tpu as pltpu
from jax.sharding import PartitionSpec as P

NX, NY, NZ = 4, 8, 8
F32, BF16 = jnp.float32, jnp.bfloat16
precise = lax.Precision.HIGHEST


def dev(row, col):
    return {"row": row, "col": col}


def fdot(a, b):
    return jnp.dot(a, b, preferred_element_type=F32, precision=precise)


def tdot(a, b):
    return lax.dot_general(a, b, (((0,), (0,)), ((), ())), preferred_element_type=F32, precision=precise)


def wait_bytes(ref, sem):
    pltpu.make_async_copy(ref, ref, sem).wait()


def listed(struct_ref, block):
    hit = jnp.where(struct_ref[...] == block, 1.0, 0.0)
    return jnp.max(hit, axis=1, keepdims=True)


def kernel(
    s_hbm, p1_hbm, p2_hbm, link_hbm, inv1_hbm, inv2_hbm, st1_hbm, st2_hbm,
    out,
    st1, st2, s_v, link_v, inv_v, wide, tall, gram1, gram2, p_v, rows_z, rows_x, ordered, fac_t, late_t, raw, fac,
    q_out, q_in, q_x, q_xin, part_out, part_in, summed, z_out, z_in,
    ea_own, ea_twin, ea_out, ea_in, ea_z, ea_zin, ea_y, ea_yin, ea_sum,
    eb_own, eb_twin, eb_out, eb_in, eb_z, eb_zin, eb_y, eb_yin, eb_sum, rest, carry,
    load_sem, a_send, send_sem, recv_sem,
):
    row, col = lax.axis_index("row"), lax.axis_index("col")
    col1, col2 = out.at[pl.ds(0, 6)], out.at[pl.ds(6, 6)]
    diag1, link, diag2 = out.at[12], out.at[13], out.at[14]
    y, core = lax.div(row, 2), lax.rem(row, 2)
    z, x = lax.div(col, NX), lax.rem(col, NX)
    part = lax.rem(lax.rem(z, 4) + 2 + lax.div(lax.rem(col, 16), 2) + 4 - lax.rem(y, 4), 4)

    loads = [
        pltpu.make_async_copy(p1_hbm, p_v.at[0], load_sem.at[0]),
        pltpu.make_async_copy(p2_hbm, p_v.at[1], load_sem.at[1]),
        pltpu.make_async_copy(inv1_hbm, inv_v.at[0], load_sem.at[2]),
        pltpu.make_async_copy(inv2_hbm, inv_v.at[1], load_sem.at[3]),
        pltpu.make_async_copy(link_hbm, link_v, load_sem.at[4]),
        pltpu.make_async_copy(st1_hbm, st1, load_sem.at[6]),
        pltpu.make_async_copy(st2_hbm, st2, load_sem.at[7]),
        pltpu.make_async_copy(s_hbm, s_v, load_sem.at[5]),
    ]
    for load in loads:
        load.start()

    barrier = pltpu.get_barrier_semaphore()

    def greet(r, c):
        pl.semaphore_signal(barrier, inc=1, device_id=dev(r, c), device_id_type=pl.DeviceIdType.MESH)

    src_row = lax.rem(col, 16)
    for slot in range(4):
        src_col = 4 * (4 * core + part) + slot
        me = jnp.logical_and(src_row == row, src_col == col)

        @pl.when(jnp.logical_not(me))
        def _():
            greet(src_row, src_col)

    for d in range(1, NZ):
        greet(row, 4 * lax.rem(z + d, NZ) + x)
    for d in range(1, NX):
        greet(row, 4 * z + lax.rem(x + d, NX))
    for d in range(1, NY):
        greet(2 * lax.rem(y + d, NY) + core, col)
    twin = 2 * y + 1 - core
    greet(twin, col)

    targets = []
    others = 3 + 7 + 7 + 1
    for zhi in range(2):
        for k in range(2):
            r_t = 2 * (lax.rem(y + 10 - z + lax.div(row, 4), 4) + 4 * k) + lax.div(z, 4)
            c_t = row + 16 * zhi
            me = jnp.logical_and(r_t == row, c_t == col)
            others = others + jnp.where(me, 0, 1)
            targets.append((zhi, k, r_t, c_t, me))
    for load in loads[:-1]:
        load.wait()
    structs = (st1, st2)
    uppers = [inv_v[sn].astype(BF16) for sn in range(2)]
    for sn in range(2):
        lower = (inv_v[sn] - uppers[sn].astype(F32)).astype(BF16)
        rows = jnp.concatenate([
            p_v[sn, block // 2, block % 2].astype(F32) * listed(structs[sn], block * 16 + row) for block in range(6)
        ], axis=0).astype(BF16)
        product = (jnp.dot(rows, uppers[sn], preferred_element_type=F32)
                   + jnp.dot(rows, lower, preferred_element_type=F32))
        rows_z[z, sn] = product.reshape(3, 2, 8, 256).astype(BF16)
    rows_x[x] = rows_z[z, 1]
    pl.semaphore_wait(barrier, others)

    spot_a = raw.at[:, :, lax.div(z, 4), lax.rem(z, 4), x]

    def stage_a(zhi, k, r_t, c_t):
        return pltpu.make_async_remote_copy(
            rows_z.at[z, :, :, zhi], spot_a, a_send.at[2 * zhi + k], recv_sem.at[0, 0],
            device_id=dev(r_t, c_t), device_id_type=pl.DeviceIdType.MESH)

    for zhi, k, r_t, c_t, me in targets:
        @pl.when(jnp.logical_not(me))
        def _():
            stage_a(zhi, k, r_t, c_t).start()

        @pl.when(me)
        def _():
            pltpu.make_async_copy(rows_z.at[z, :, :, zhi], spot_a, recv_sem.at[0, 0]).start()

    def remote(src, dst, stage, sn, r, c):
        pltpu.make_async_remote_copy(
            src, dst, send_sem.at[stage, sn], recv_sem.at[stage, sn],
            device_id=dev(r, c), device_id_type=pl.DeviceIdType.MESH).start()

    wait_bytes(raw.at[:, :, core, part], recv_sem.at[0, 0])
    for sn in range(2):
        spot = raw.at[sn, :, core, part]
        for d, at in ((2, 0), (6, 2)):
            near = raw.at[sn, :, core, part, pl.ds(at, 2)]
            remote(near, near, 1, sn, 2 * lax.rem(y + d, NY) + core, col)
        for d in (1, 7):
            remote(spot, spot, 1, sn, 2 * lax.rem(y + d, NY) + core, col)
    for d in (4, 3, 5, 2, 6, 1, 7):
        remote(rows_z.at[z], rows_z.at[z], 5, 0, row, 4 * lax.rem(z + d, NZ) + x)
    for d in (2, 1, 3):
        remote(rows_x.at[x], rows_x.at[x], 14, 0, row, 4 * z + lax.rem(x + d, NX))
    wide[...] = fdot(link_v[...].astype(F32), inv_v[1])
    for sn in range(2):
        wait_bytes(raw.at[sn, :, core, pl.ds(0, 3)], recv_sem.at[1, sn])
        spot = raw.at[sn, :, core]
        remote(spot, spot, 2, sn, twin, col)
    loads[-1].wait()

    for sn in range(2):
        wait_bytes(raw.at[sn, :, core], recv_sem.at[2, sn])
        for b in range(3):
            fac[sn, b] = raw[sn, b].astype(F32).reshape(256, 256).astype(BF16)
        for half in ((0, 1) if sn == 0 else (1, 0)):
            def block_row(step, _):
                a = 3 * half + step
                total = jnp.dot(s_v[a, 0], fac[sn, 0], preferred_element_type=F32)
                total += jnp.dot(s_v[a, 1], fac[sn, 1], preferred_element_type=F32)
                total += jnp.dot(s_v[a, 2], fac[sn, 2], preferred_element_type=F32)
                for xd in range(NX):
                    for zd in range(NZ):
                        at = 8 * (4 * zd + xd)
                        piece = total[at:at + 8, :].astype(BF16)
                        if sn and half:
                            q_out[zd, xd, step] = piece
                        else:
                            part_out[2 * sn + half, xd, zd, step] = piece
                return 0

            lax.fori_loop(0, 3, block_row, 0)
            if sn and half:
                for d in (4, 3, 5, 2, 6, 1, 7):
                    to = lax.rem(z + d, NZ)
                    remote(q_out.at[to], q_in.at[d - 1], 12, 0, row, 4 * to + x)
            else:
                n = 2 * sn + half
                for d in (2, 1, 3):
                    to = lax.rem(x + d, NX)
                    remote(part_out.at[n, to], part_in.at[n, d - 1], 3 + half, sn, row, 4 * z + to)

    wait_bytes(rows_z.at[pl.ds(0, 7)], recv_sem.at[5, 0])
    wait_bytes(rows_x.at[pl.ds(0, 3)], recv_sem.at[14, 0])
    for sn in range(2):
        for block in range(6):
            ordered[block // 3, :, block % 3] = rows_z[:, sn, block // 2, block % 2].astype(F32)
        fac_t[sn] = ordered[...].reshape(384, 256).T.astype(BF16)
    blank = jnp.zeros((32, 256), F32)
    late = jnp.stack([rows_x[:, block // 2, block % 2].astype(F32) for block in (3, 4, 5)], axis=1)
    late_t[...] = jnp.concatenate([late.reshape(96, 256), blank], axis=0).T.astype(BF16)
    tall[...] = wide[...].T
    gram1[...] = tdot(inv_v[0], inv_v[0])
    gram2[...] = tdot(inv_v[1], inv_v[1]) + fdot(tall[...], fdot(gram1[...], wide[...]))

    def spread_rows(to, m, matrix):
        for xd in range(NX):
            for zd in range(NZ):
                at = 8 * (4 * zd + xd)
                for lanes in range(2):
                    to[lanes, xd, zd, m] = matrix[at:at + 8, 128 * lanes:128 * lanes + 128]

    groups = ((ea_own, ea_twin, ea_out, ea_in, ea_z, ea_zin, ea_y, ea_yin, ea_sum),
              (eb_own, eb_twin, eb_out, eb_in, eb_z, eb_zin, eb_y, eb_yin, eb_sum))

    def send_z(n, half, sn):
        for d in (4, 3, 5, 2, 6, 1, 7):
            to = lax.rem(z + d, NZ)
            remote(z_out.at[n, to], z_in.at[n, d - 1], 7 + 8 * half, sn, row, 4 * to + x)

    def sum_x(g):
        g_out, g_in, g_z, g_zin = groups[g][2:6]
        wait_bytes(g_in, recv_sem.at[8, g])
        total = g_out[x].astype(F32)
        for d in range(3):
            total += g_in[d].astype(F32)
        g_z[...] = total.astype(BF16)
        for d in (4, 3, 5, 2, 6, 1, 7):
            to = lax.rem(z + d, NZ)
            remote(g_z.at[to], g_zin.at[d - 1], 9, g, row, 4 * to + x)

    def sum_z(g):
        g_z, g_zin, g_y, g_yin = groups[g][4:8]
        wait_bytes(g_zin, recv_sem.at[9, g])
        total = g_z[z].astype(F32)
        for d in range(7):
            total += g_zin[d].astype(F32)
        g_y[...] = total
        for d in (4, 3, 5, 2, 6, 1, 7):
            remote(g_y, g_yin.at[d - 1], 10, g, 2 * lax.rem(y + d, NY) + core, col)

    for sn in range(2):
        for half in range(2 - sn):
            n = 2 * sn + half
            wait_bytes(part_in.at[n], recv_sem.at[3 + half, sn])
            total = part_out[n, x].astype(F32)
            for d in range(3):
                total += part_in[n, d].astype(F32)
            summed[half] = total
            z_out[n] = total.astype(BF16)
            if sn == 0:
                send_z(n, half, sn)
        depth = 384 - 192 * sn
        sums = (summed[...] if sn == 0 else summed[0]).reshape(depth, 256)
        high = sums.astype(BF16)
        low = (sums - high.astype(F32)).astype(BF16)

        def part_sum(which):
            factor = fac_t[which, :, 0:depth]
            return -(jnp.dot(factor, high, preferred_element_type=F32)
                     + jnp.dot(factor, low, preferred_element_type=F32))

        g_own, g_twin, g_out, g_in = groups[sn][:4]
        if sn == 0:
            first = part_sum(0)
            top_t = part_sum(1)
            top = top_t.T
            spread_rows(g_own, 0, first)
            spread_rows(g_own, 1, top)
        else:
            second = part_sum(1) + rest[...]
            wait_bytes(q_in, recv_sem.at[12, 0])
            total = q_out[z].astype(F32)
            for d in range(7):
                total += q_in[d].astype(F32)
            q_x[...] = total.astype(BF16)
            sums = jnp.concatenate([total.reshape(96, 256), blank], axis=0)
            high = sums.astype(BF16)
            low = (sums - high.astype(F32)).astype(BF16)
            second -= (jnp.dot(late_t[...], high, preferred_element_type=F32)
                       + jnp.dot(late_t[...], low, preferred_element_type=F32))
            spread_rows(g_own, 0, second)
        remote(g_own.at[1 - core], g_twin, 6, sn, twin, col)
        if sn:
            send_z(2, 0, 1)
            for d in (2, 1, 3):
                to = lax.rem(x + d, NX)
                remote(q_x.at[to], q_xin.at[d - 1], 13, 0, row, 4 * z + to)
        if sn == 0:
            rest[...] = fdot(tall[...], fdot(first, wide[...]) - top) - fdot(top_t, wide[...])
        wait_bytes(g_twin, recv_sem.at[6, sn])
        g_out[...] = (g_own[core] + g_twin[...]).astype(BF16)
        for d in (2, 1, 3):
            to = lax.rem(x + d, NX)
            remote(g_out.at[to], g_in.at[d - 1], 8, sn, row, 4 * z + to)

    sum_x(0)
    sum_x(1)
    sum_z(0)

    def z_total(n, stage, sn):
        wait_bytes(z_in.at[n], recv_sem.at[stage, sn])
        total = z_out[n, z].astype(F32)
        for d in range(7):
            total += z_in[n, d].astype(F32)
        return total

    for half in range(2):
        total = z_total(half, 7 + 8 * half, 0)
        for step in range(3):
            block = 3 * half + step
            col1[block] = total[step] * (-listed(st1, block * 16 + row))
    carry[...] = fdot(col1[...].reshape(48, 256), wide[...])
    sum_z(1)

    early = z_total(2, 7, 1)
    wait_bytes(q_xin, recv_sem.at[13, 0])
    late = q_x[x].astype(F32)
    for d in range(3):
        late += q_xin[d].astype(F32)
    for block in range(6):
        total = (early if block < 3 else late)[block % 3] + carry[8 * block:8 * block + 8, :]
        col2[block] = total * (-listed(st2, block * 16 + row))

    at = pl.multiple_of(8 * col, 8)

    def whole(g, m):
        g_sum = groups[g][8]
        return jnp.concatenate([g_sum[0, m], g_sum[1, m]], axis=1)

    def sum_y(g):
        g_y, g_yin, g_sum = groups[g][6:9]
        wait_bytes(g_yin, recv_sem.at[10, g])
        total = g_y[...]
        for d in range(7):
            total += g_yin[d]
        g_sum[core] = total
        remote(g_sum.at[core], g_sum.at[core], 11, g, twin, col)

    for zhi, k, r_t, c_t, me in targets:
        @pl.when(jnp.logical_not(me))
        def _():
            stage_a(zhi, k, r_t, c_t).wait_send()

    wait_bytes(rows_z.at[pl.ds(0, 7)], send_sem.at[5, 0])
    wait_bytes(rows_x.at[pl.ds(0, 3)], send_sem.at[14, 0])
    wait_bytes(q_in, send_sem.at[12, 0])
    wait_bytes(q_xin, send_sem.at[13, 0])
    for sn in range(2):
        wait_bytes(raw.at[sn, :, core, pl.ds(0, 3)], send_sem.at[1, sn])
        wait_bytes(raw.at[sn, :, core], send_sem.at[2, sn])
        for half in range(2 - sn):
            wait_bytes(part_in.at[2 * sn + half], send_sem.at[3 + half, sn])
            wait_bytes(z_in.at[2 * sn + half], send_sem.at[7 + 8 * half, sn])
        wait_bytes(groups[sn][1], send_sem.at[6, sn])
        wait_bytes(groups[sn][3], send_sem.at[8, sn])
        wait_bytes(groups[sn][5], send_sem.at[9, sn])

    sum_y(0)
    wait_bytes(ea_sum.at[core], recv_sem.at[11, 0])
    diag1[...] = gram1[pl.ds(at, 8), :] - whole(0, 0)
    link[...] = -(whole(0, 1) + fdot(diag1[...], wide[...]))
    sum_y(1)
    wait_bytes(eb_sum.at[core], recv_sem.at[11, 1])
    diag2[...] = gram2[pl.ds(at, 8), :] - whole(1, 0)

    for sn in range(2):
        wait_bytes(groups[sn][7], send_sem.at[10, sn])
        wait_bytes(groups[sn][8].at[core], send_sem.at[11, sn])


def body(stored_inverse, panel_first, panel_second, panel_link, inv_first, inv_second, struct_first, struct_second):
    anywhere = pl.BlockSpec(memory_space=pl.ANY)
    vmem = pl.BlockSpec(memory_space=pltpu.VMEM)

    def e_scratch(n):
        return [
            pltpu.VMEM((2, 4, 8, n, 8, 128), F32), pltpu.VMEM((4, 8, n, 8, 128), F32),
            pltpu.VMEM((4, 8, n, 8, 128), BF16), pltpu.VMEM((3, 8, n, 8, 128), BF16),
            pltpu.VMEM((8, n, 8, 128), BF16), pltpu.VMEM((7, n, 8, 128), BF16),
            pltpu.VMEM((n, 8, 128), F32), pltpu.VMEM((7, n, 8, 128), F32), pltpu.VMEM((2, n, 8, 128), F32),
        ]

    out = pl.pallas_call(
        kernel,
        out_shape=jax.ShapeDtypeStruct((15, 8, 256), F32),
        in_specs=[anywhere] * 8,
        out_specs=vmem,
        scratch_shapes=[
            pltpu.VMEM(struct_first.reshape(1, -1).shape, jnp.int32),
            pltpu.VMEM(struct_second.reshape(1, -1).shape, jnp.int32),
            pltpu.VMEM((6, 3, 256, 256), BF16),
            pltpu.VMEM((256, 256), BF16),
            pltpu.VMEM((2, 256, 256), F32),
            pltpu.VMEM((256, 256), F32),
            pltpu.VMEM((256, 256), F32),
            pltpu.VMEM((256, 256), F32),
            pltpu.VMEM((256, 256), F32),
            pltpu.VMEM((2, 3, 2, 8, 256), BF16),
            pltpu.VMEM((8, 2, 3, 2, 8, 256), BF16),
            pltpu.VMEM((4, 3, 2, 8, 256), BF16),
            pltpu.VMEM((2, 8, 3, 8, 256), F32),
            pltpu.VMEM((2, 256, 384), BF16),
            pltpu.VMEM((256, 128), BF16),
            pltpu.VMEM((2, 3, 2, 4, 4, 8, 256), BF16),
            pltpu.VMEM((2, 3, 256, 256), BF16),
            pltpu.VMEM((8, 4, 3, 8, 256), BF16),
            pltpu.VMEM((7, 4, 3, 8, 256), BF16),
            pltpu.VMEM((4, 3, 8, 256), BF16),
            pltpu.VMEM((3, 3, 8, 256), BF16),
            pltpu.VMEM((3, 4, 8, 3, 8, 256), BF16),
            pltpu.VMEM((3, 3, 8, 3, 8, 256), BF16),
            pltpu.VMEM((2, 8, 3, 8, 256), F32),
            pltpu.VMEM((3, 8, 3, 8, 256), BF16),
            pltpu.VMEM((3, 7, 3, 8, 256), BF16),
            *e_scratch(2),
            *e_scratch(1),
            pltpu.VMEM((256, 256), F32),
            pltpu.VMEM((48, 256), F32),
            pltpu.SemaphoreType.DMA((8,)),
            pltpu.SemaphoreType.DMA((8,)),
            pltpu.SemaphoreType.DMA((16, 2)),
            pltpu.SemaphoreType.DMA((16, 2)),
        ],
        compiler_params=pltpu.CompilerParams(
            collective_id=0, has_side_effects=True, vmem_limit_bytes=40 * 1024 * 1024),
    )(
        *[pltpu.with_memory_space_constraint(v, pltpu.HBM) for v in (
            stored_inverse.reshape(6, 3, 256, 256),
            panel_first.reshape(3, 2, 8, 256),
            panel_second.reshape(3, 2, 8, 256),
            panel_link, inv_first, inv_second,
            struct_first.reshape(1, -1), struct_second.reshape(1, -1),
        )])
    c1, c2, d1, lk, d2 = out[:6], out[6:12], out[12], out[13], out[14]
    return c1.reshape(6, 1, 8, 256), c2.reshape(6, 1, 8, 256), d1, lk, d2


def solution(mesh):
    return jax.shard_map(
        body,
        mesh=mesh,
        in_specs=(P(None, "row", None, "col", None, None), P(None, "row", "col", None), P(None, "row", "col", None),
                  P(), P(), P(), P(), P()),
        out_specs=(P(None, "row", "col", None), P(None, "row", "col", None), P("col", None), P("col", None), P("col", None)),
        check_vma=False,
    )
```
